32 devices in a mesh: grp: 2 (over x), chan: 16 (over z, y, core).
Axes of the slice: x: 2, y: 2, z: 4, core: 2. Of those that a mesh axis runs over, the one named last changes fastest.
Arguments:
- voltages: bfloat16 [2, 1024, 2, 32, 512], P(None, 'chan', None, None, 'grp'), parts along dimension 4, may hold values from -80 to 80
- gains: float32 [2, 2, 1024], P(None, None, 'chan'), may hold values from -1 to 1
- feed_cyl: int32 [1024], replicated, may hold values from 0 to 3, as said below
- feed_ns: int32 [1024], replicated, may hold values from 0 to 255
- ew_index: int32 [4, 4], replicated, may hold values from 0 to 63
- ns_beam: int32 [256], replicated, may hold values from 0 to 511
Outputs:
- intensity: float32 [1024, 8, 512], P('chan', 'grp'), parts along dimension 1
The draws below stay inside these ranges and needn't reach their ends.
There are 2 independent parts, one for each index of `grp`. The reference program is written for one: setup_inputs(seed, part) draws one part's arguments, and reference() takes and returns one part's arrays. A program takes and returns all parts, laid end to end along the dimension named above; an argument that names none is the same for every part. Nothing has to cross between parts.
Inputs may be any that keep to these rules, and one draw needn't show every extreme that they name: Together, feed_cyl and feed_ns name every pair of a cylinder and a north-south position exactly once.
All inputs are finite; a program needn't handle non-finite values.
Results may differ from the reference program's by a relative error of at most 0.0018.
Values may be sent and summed in bfloat16 or wider, within the bound.
A program may use at most 128 MiB of HBM per device.

```python
import math
import jax
import jax.numpy as jnp
from jax import lax

CYL = 4
NSF = 256
POL = 2
EWB = 4
NSB = 256
EW_PH = 64
UP = 16
DS = 4
TS = 256
FEEDS = 1024
BEAMS = 1024
CH = 32
TOUT = 4


def draw_voltages(key, part):
    key_base, key_spread = jax.random.split(key, 2)
    chan_index = jnp.arange(CH, dtype=jnp.float32)
    spread = jnp.exp(jax.random.uniform(key_spread, (CH,), dtype=jnp.float32) * jnp.log(10.0))
    rise_curve = 1.0 + 2.0 * chan_index / max(CH - 1, 1)
    noise_part = jnp.clip(jax.random.normal(key_base, (2, FEEDS, POL, CH, TS), dtype=jnp.float32), -4.0, 4.0)
    amplitude = jnp.sqrt(rise_curve * spread)
    return (noise_part * amplitude[None, None, None, :, None]).astype(jnp.bfloat16)


def feed_layout(key):
    return jax.random.permutation(jax.random.fold_in(key, 11), FEEDS).astype(jnp.int32)


def draw_feed_cyl(key, part):
    return (feed_layout(key) // NSF).astype(jnp.int32)


def draw_feed_ns(key, part):
    return (feed_layout(key) % NSF).astype(jnp.int32)


def touch_ends(entries, own_key, least, high):
    longest = entries.shape.index(max(entries.shape))
    spots = []
    for shift in (0, 1):
        where = [jax.random.randint(jax.random.fold_in(own_key, axis), (), 0, length) for axis, length in enumerate(entries.shape)]
        where[longest] = (where[longest] + shift) % entries.shape[longest]
        spots.append(tuple(where))
    return entries.at[spots[0]].set(least).at[spots[1]].set(high)


def levels(rng, extent, shards, smallest, high):
    factor_of = 1.0
    for dim, parts in shards:
        heights = jax.random.uniform(jax.random.fold_in(jax.random.fold_in(rng, 6), dim), (parts,), jnp.float32, smallest / len(shards), high / len(shards))
        factor_of = factor_of * jnp.repeat(jnp.exp(heights), extent[dim] // parts).reshape((-1,) + (1,) * (len(extent) - 1 - dim))
    return factor_of


def setup_inputs(seed: int = 0, part: int = 0) -> dict:
    keys = jax.random.split(jax.random.key(seed), 7)
    own_keys = jax.random.split(jax.random.fold_in(keys[6], part), 7)
    return {
        "voltages": draw_voltages(jax.random.fold_in(jax.random.fold_in(keys[6], part), 71), part),
        "gains": jnp.clip(jax.random.uniform(keys[1], (2, POL, FEEDS), jnp.float32, -1.0, 1.0) * levels(keys[1], (2, POL, FEEDS), ((2, 16),), -0.4, 0.0), -1.0, 1.0),
        "feed_cyl": draw_feed_cyl(jax.random.fold_in(keys[6], 71), part),
        "feed_ns": draw_feed_ns(jax.random.fold_in(keys[6], 71), part),
        "ew_index": touch_ends(jax.random.randint(keys[4], (EWB, CYL), 0, EW_PH), jax.random.fold_in(keys[4], 1), 0, EW_PH - 1).astype(jnp.int32),
        "ns_beam": touch_ends(jax.random.randint(keys[5], (NSB,), 0, 2 * NSF), jax.random.fold_in(keys[5], 1), 0, (2 * NSF) - 1).astype(jnp.int32),
    }


eps_power = 1e-6


def phase_table(feed_cyl, feed_ns, ew_index, ns_beam):
    modulus = 2 * NSF * EW_PH
    cyl_onehot = (feed_cyl[:, None] == jnp.arange(CYL, dtype=jnp.int32)[None, :]).astype(jnp.int32)
    ew_term = jnp.sum(cyl_onehot[:, None, :] * ew_index[None, :, :], axis=2)
    ns_term = feed_ns[:, None] * ns_beam[None, :] * EW_PH
    steps_int = (ew_term[:, :, None] * (2 * NSF) + ns_term[:, None, :]) % modulus
    angles = steps_int.reshape(FEEDS, EWB * NSB).astype(jnp.float32) * (2.0 * math.pi / modulus)
    cosine = jnp.cos(angles).astype(jnp.bfloat16)
    sine_part = jnp.sin(angles).astype(jnp.bfloat16)
    upper_rows = jnp.concatenate([cosine, sine_part], axis=1)
    lower_rows = jnp.concatenate([-sine_part, cosine], axis=1)
    return jnp.concatenate([upper_rows, lower_rows], axis=0)


def upchannel_table():
    bin_index = jnp.arange(UP, dtype=jnp.int32)
    angles = ((bin_index[:, None] * bin_index[None, :]) % UP).astype(jnp.float32) * (2.0 * math.pi / UP)
    cosine = jnp.cos(angles)
    sine_part = jnp.sin(angles)
    return jnp.stack([jnp.stack([cosine, -sine_part], -1), jnp.stack([sine_part, cosine], -1)], 1)


def reference(voltages, gains, feed_cyl, feed_ns, ew_index, ns_beam):
    weights = phase_table(feed_cyl, feed_ns, ew_index, ns_beam)
    fine_table = upchannel_table()
    gain_real = gains[0].T[:, :, None]
    gain_imag = gains[1].T[:, :, None]

    def one_channel(channel):
        sample = lax.dynamic_index_in_dim(voltages, channel, 3, keepdims=False).astype(jnp.float32)
        cal_real = (gain_real * sample[0] - gain_imag * sample[1]).astype(jnp.bfloat16)
        cal_imag = (gain_real * sample[1] + gain_imag * sample[0]).astype(jnp.bfloat16)
        beam_list = []
        for polarity in range(POL):
            stacked = jnp.concatenate([cal_real[:, polarity, :].T, cal_imag[:, polarity, :].T], axis=1)
            beam_list.append(jnp.dot(stacked, weights, preferred_element_type=jnp.float32))
        beam_sums = jnp.stack(beam_list).reshape(POL, TOUT, DS, UP, 2, BEAMS)
        fine_bins = jnp.einsum("pudjrb,jrks->pbudks", beam_sums, fine_table, precision=lax.Precision.HIGHEST)
        return jnp.sum(fine_bins * fine_bins, axis=(0, 3, 5))

    beam_power = lax.map(one_channel, jnp.arange(CH, dtype=jnp.int32))
    beam_power = jnp.transpose(beam_power, (1, 2, 0, 3))
    baseline = jnp.mean(beam_power, axis=(2, 3))
    intensity = beam_power / (baseline[:, :, None, None] + eps_power)
    return intensity.reshape(BEAMS, TOUT, CH * UP)
```

```python
import functools
import math

import jax
import jax.numpy as jnp
import numpy as np
from jax import lax
from jax.experimental import pallas as pl
from jax.experimental.pallas import tpu as pltpu
from jax.sharding import PartitionSpec as P

CYL = 4
NSF = 256
EWB = 4
NSB = 256
EW_PH = 64
UP = 16
DS = 4
FEEDS = 1024
BEAMS = 1024
TOUT = 4


eps_power = 1e-06
MESH = pl.DeviceIdType.MESH


def phase_table(feed_cyl, feed_ns, ew_index, ns_beam):
    modulus = 2 * NSF * EW_PH
    cyl_onehot = (feed_cyl[:, None] == jnp.arange(CYL, dtype=jnp.int32)[None, :]).astype(jnp.int32)
    ew_term = jnp.sum(cyl_onehot[:, None, :] * ew_index[None, :, :], axis=2)
    ns_term = feed_ns[:, None] * ns_beam[None, :] * EW_PH
    steps_int = (ew_term[:, :, None] * (2 * NSF) + ns_term[:, None, :]) % modulus
    angles = steps_int.reshape(FEEDS, EWB * NSB).astype(jnp.float32) * (2.0 * math.pi / modulus)
    cosine = jnp.cos(angles).astype(jnp.bfloat16)
    sine_part = jnp.sin(angles).astype(jnp.bfloat16)
    upper_rows = jnp.concatenate([cosine, sine_part], axis=1)
    lower_rows = jnp.concatenate([-sine_part, cosine], axis=1)
    return jnp.concatenate([upper_rows, lower_rows], axis=0)


def upchannel_table():
    bin_index = jnp.arange(UP, dtype=jnp.int32)
    angles = (bin_index[:, None] * bin_index[None, :] % UP).astype(jnp.float32) * (
        2.0 * math.pi / UP
    )
    cosine = jnp.cos(angles)
    sine_part = jnp.sin(angles)
    return jnp.stack([jnp.stack([cosine, -sine_part], -1), jnp.stack([sine_part, cosine], -1)], 1)


def shards(voltages, gains, feed_cyl, feed_ns, ew_index, ns_beam):
    weights = phase_table(feed_cyl, feed_ns, ew_index, ns_beam).reshape(2, FEEDS, 2 * BEAMS)
    fine_table = upchannel_table()
    sample = voltages.astype(jnp.float32)
    gain_real = gains[0].T[:, :, None, None]
    gain_imag = gains[1].T[:, :, None, None]
    calibrated = jnp.stack(
        [
            (gain_real * sample[0] - gain_imag * sample[1]).astype(jnp.bfloat16),
            (gain_real * sample[1] + gain_imag * sample[0]).astype(jnp.bfloat16),
        ]
    )
    arrived = lax.all_to_all(calibrated, "chan", split_axis=3, concat_axis=1, tiled=True)
    pieces = arrived.shape[2]
    channels = arrived.shape[3]
    beam_sums = jnp.einsum("rfpct,rfq->pctq", arrived, weights, preferred_element_type=jnp.float32)
    beam_sums = beam_sums.reshape(pieces, channels, TOUT, DS, UP, 2, BEAMS)
    fine_bins = jnp.einsum(
        "pcudjrb,jrks->pbudcks", beam_sums, fine_table, precision=lax.Precision.HIGHEST
    )
    beam_power = jnp.sum(jnp.sum(fine_bins * fine_bins, axis=(3, 6)), axis=0)
    total_chans = beam_power.shape[2] * lax.axis_size("chan")
    band_sum = lax.psum(jnp.sum(beam_power, axis=(2, 3)), "chan")
    baseline = band_sum / (total_chans * UP)
    normed = beam_power / (baseline[:, :, None, None] + eps_power)
    intensity = lax.all_to_all(normed, "chan", split_axis=0, concat_axis=2, tiled=True)
    return intensity.reshape(intensity.shape[0], TOUT, intensity.shape[2] * UP)

def fft(values):
    size = len(values)
    if size == 1:
        return values
    even = fft(values[0::2])
    odd = fft(values[1::2])
    low, high = [], []
    for k in range(size // 2):
        er, ei = even[k]
        xr, xi = odd[k]
        if k == 0:
            tr, ti = xr, xi
        elif 4 * k == size:
            tr, ti = xi, -xr
        else:
            c = math.cos(2.0 * math.pi * k / size)
            s = math.sin(2.0 * math.pi * k / size)
            if 8 * k == size:
                tr, ti = (xr + xi) * c, (xi - xr) * c
            elif 8 * k == 3 * size:
                tr, ti = (xi - xr) * s, -(xr + xi) * s
            else:
                tr, ti = xr * c + xi * s, xi * c - xr * s
        low.append((er + tr, ei + ti))
        high.append((er - tr, ei - ti))
    return low + high


def cos_sin(steps):
    quarter = (steps + 64) >> 7
    x = (steps - (quarter << 7)).astype(jnp.float32) * (2.0 * math.pi / 512)
    y = x * x
    s = x * (1.0 + y * (-1 / 6 + y * (1 / 120 + y * (-1 / 5040 + y * (1 / 362880)))))
    c = 1.0 + y * (-0.5 + y * (1 / 24 + y * (-1 / 720 + y * (1 / 40320))))
    odd = (quarter & 1) == 1
    cosine = jnp.where(odd, s, c)
    sine = jnp.where(odd, c, s)
    cosine = jnp.where(((quarter + 1) & 2) == 2, -cosine, cosine)
    sine = jnp.where((quarter & 2) == 2, -sine, sine)
    return cosine, sine


def calibrate_kernel(volt_ref, gain_ref, spread_ref, out_ref):
    half = volt_ref.shape[1] // 2
    halves = []
    for p in range(2):
        real = volt_ref[p, :half, :].astype(jnp.float32)
        imag = volt_ref[p, half:, :].astype(jnp.float32)
        gr = gain_ref[p, :half, :]
        gi = gain_ref[p, half:, :]
        both = jnp.concatenate(
            [
                (gr * real - gi * imag).astype(jnp.bfloat16),
                (gr * imag + gi * real).astype(jnp.bfloat16),
            ],
            axis=0,
        )
        turned = lax.dot_general(
            spread_ref[...], both, (((1,), (1,)), ((), ())), preferred_element_type=jnp.float32
        )
        halves.append(turned.reshape(TOUT * UP, 1, 8, 2 * half))
    rows = jnp.concatenate(halves, axis=1).astype(jnp.bfloat16)
    out_ref[0] = rows.reshape(TOUT, UP * 16, 2 * half)


def beam_kernel(
    n, x_ref, ns_ref, ew_ref, nb_ref, out_ref,
    recv, wre, wim, sums, psc, pbuf, precv, turn,
    send_sem, recv_sem, own_sem, psend_sem, precv_sem, pown_sem,
):
    me = lax.axis_index("chan")
    barrier = pltpu.get_barrier_semaphore()

    def greet(s, carry):
        pl.semaphore_signal(
            barrier, inc=1, device_id={"chan": lax.rem(me + s, n)}, device_id_type=MESH
        )
        return carry

    lax.fori_loop(1, n, greet, 0)
    pl.semaphore_wait(barrier, n - 1)

    mine = pl.ds(pl.multiple_of(me * 128, 128), 128)

    def volt_copy(u, s):
        d = lax.rem(me + s, n)
        return pltpu.make_async_remote_copy(
            src_ref=x_ref.at[d, u],
            dst_ref=recv.at[u, :, mine],
            send_sem=send_sem.at[u, s],
            recv_sem=recv_sem.at[u, s],
            device_id={"chan": d},
            device_id_type=MESH,
        )

    def own_copy(u):
        return pltpu.make_async_copy(x_ref.at[me, u], recv.at[u, :, mine], own_sem.at[u])

    def power_copy(u, s):
        d = lax.rem(me + s, n)
        return pltpu.make_async_remote_copy(
            src_ref=pbuf.at[u, d],
            dst_ref=precv.at[u, me],
            send_sem=psend_sem.at[u, s],
            recv_sem=precv_sem.at[u, s],
            device_id={"chan": d},
            device_id_type=MESH,
        )

    def own_power(u):
        return pltpu.make_async_copy(pbuf.at[u, me], precv.at[u, me], pown_sem.at[u])

    def each(make, act, u):
        def one(s, carry):
            getattr(make(u, s), act)()
            return carry

        lax.fori_loop(1, n, one, 0)

    for u in range(TOUT):
        each(volt_copy, "start", u)
    for u in range(TOUT):
        own_copy(u).start()

    def table(s, carry):
        feeds = pl.ds(pl.multiple_of(s * 64, 64), 64)
        top = pl.ds(pl.multiple_of(s * 128, 128), 64)
        low = pl.ds(pl.multiple_of(s * 128 + 64, 64), 64)
        slope = ns_ref[feeds, :] * nb_ref[...]
        for e in range(EWB):
            cosine, sine = cos_sin((slope + ew_ref[feeds, e : e + 1]) & 511)
            cols = slice(e * NSB, (e + 1) * NSB)
            cosine = cosine.astype(jnp.bfloat16)
            wre[top, cols] = cosine
            wim[low, cols] = cosine
            wim[top, cols] = sine.astype(jnp.bfloat16)
            wre[low, cols] = (-sine).astype(jnp.bfloat16)
        return carry

    lax.fori_loop(0, n, table, 0)
    left = lax.broadcasted_iota(jnp.int32, (16, 128), 1) < 64

    for u in range(TOUT):
        each(volt_copy, "wait_recv", u)
        own_copy(u).wait()

        def block(nb, carry, u=u):
            cols = pl.ds(pl.multiple_of(nb * 256, 256), 256)
            sums[0] = jnp.dot(recv[u], wre[:, cols], preferred_element_type=jnp.float32)
            sums[1] = jnp.dot(recv[u], wim[:, cols], preferred_element_type=jnp.float32)
            for lane in range(2):
                at = slice(lane * 128, (lane + 1) * 128)
                total = None
                for p in range(2):
                    bins = fft(
                        [
                            (
                                sums[0, j * 16 + p * 8 : j * 16 + p * 8 + 8, at],
                                sums[1, j * 16 + p * 8 : j * 16 + p * 8 + 8, at],
                            )
                            for j in range(UP)
                        ]
                    )
                    power = [r * r + i * i for r, i in bins]
                    total = power if p == 0 else [a + b for a, b in zip(total, power)]
                for k in range(UP):
                    part = total[k]
                    part = part + pltpu.roll(part, 6, 0)
                    part = part + pltpu.roll(part, 7, 0)
                    psc[k : k + 1, :] = part[0:1]
                    psc[UP + k : UP + k + 1, :] = part[4:5]
                c0 = psc[:UP, :]
                c1 = psc[UP:, :]
                pair = (nb * 2 + lane) * 2
                pbuf[u, pair] = jnp.where(left, c0, pltpu.roll(c1, 64, 1)).astype(jnp.bfloat16)
                pbuf[u, pair + 1] = jnp.where(left, pltpu.roll(c0, 64, 1), c1).astype(jnp.bfloat16)
            return carry

        lax.fori_loop(0, BEAMS // 256, block, 0)
        each(power_copy, "start", u)
        own_power(u).start()

    for u in range(TOUT):
        each(volt_copy, "wait_send", u)

    for u in range(TOUT):
        each(power_copy, "wait_recv", u)
        own_power(u).wait()

        def gather(src, carry, u=u):
            rows = precv[u, src].astype(jnp.float32)
            first = pl.multiple_of(src * 32, 32)
            turn[pl.ds(first, 16), :] = rows
            turn[pl.ds(first + 16, 16), :] = pltpu.roll(rows, 64, 1)
            return carry

        lax.fori_loop(0, n, gather, 0)
        beams = jnp.concatenate(
            [turn[i * 128 : (i + 1) * 128, :].T[:64] for i in range(n * 32 // 128)], axis=1
        )
        baseline = jnp.sum(beams, axis=1, keepdims=True) / (n * 32)
        out_ref[u] = beams / (baseline + eps_power)
    for u in range(TOUT):
        each(power_copy, "wait_send", u)


def fused(n, voltages, gains, feed_cyl, feed_ns, ew_index, ns_beam):
    half = voltages.shape[1]
    samples = UP * DS * TOUT
    flat = voltages.transpose(2, 0, 1, 3, 4).reshape(2, 2 * half, -1)
    gain = gains.transpose(1, 0, 2).reshape(2, 2 * half, 1)
    row = np.arange(2 * samples)
    u, j, c, d = row // 128, row // 8 % UP, row // 4 % 2, row % DS
    take = c * samples + (u * DS + d) * UP + j
    spread = (jnp.asarray(take, jnp.int32)[:, None] == jnp.arange(2 * samples, dtype=jnp.int32)[None, :]).astype(
        jnp.bfloat16
    )
    x = pl.pallas_call(
        calibrate_kernel,
        grid=(n,),
        out_shape=jax.ShapeDtypeStruct((n, TOUT, 256, 128), jnp.bfloat16),
        in_specs=[
            pl.BlockSpec((2, 2 * half, 2 * samples), lambda i: (0, 0, i)),
            pl.BlockSpec((2, 2 * half, 1), lambda i: (0, 0, 0)),
            pl.BlockSpec((2 * samples, 2 * samples), lambda i: (0, 0)),
        ],
        out_specs=pl.BlockSpec((1, TOUT, 256, 128), lambda i: (i, 0, 0, 0)),
    )(flat, gain, spread)
    onehot = (feed_cyl[:, None] == jnp.arange(CYL, dtype=jnp.int32)[None, :]).astype(jnp.int32)
    ew = jnp.sum(onehot[:, None, :] * ew_index[None, :, :], axis=2) * 8
    vmem = pl.BlockSpec(memory_space=pltpu.VMEM)
    dma = pltpu.SemaphoreType.DMA
    out = pl.pallas_call(
        functools.partial(beam_kernel, n),
        out_shape=jax.ShapeDtypeStruct((TOUT, BEAMS // n, n * 32), jnp.float32),
        in_specs=[pl.BlockSpec(memory_space=pl.ANY), vmem, vmem, vmem],
        out_specs=vmem,
        scratch_shapes=[
            pltpu.VMEM((TOUT, 256, n * 128), jnp.bfloat16),
            pltpu.VMEM((2 * FEEDS, BEAMS), jnp.bfloat16),
            pltpu.VMEM((2 * FEEDS, BEAMS), jnp.bfloat16),
            pltpu.VMEM((2, 256, 256), jnp.float32),
            pltpu.VMEM((2 * UP, 128), jnp.float32),
            pltpu.VMEM((TOUT, n, 16, 128), jnp.bfloat16),
            pltpu.VMEM((TOUT, n, 16, 128), jnp.bfloat16),
            pltpu.VMEM((n * 32, 128), jnp.float32),
            dma((TOUT, n)), dma((TOUT, n)), dma((TOUT,)),
            dma((TOUT, n)), dma((TOUT, n)), dma((TOUT,)),
        ],
        compiler_params=pltpu.CompilerParams(
            collective_id=0, has_side_effects=True, vmem_limit_bytes=48 << 20
        ),
    )(x, feed_ns[:, None], ew, ns_beam[None, :])
    return out.transpose(1, 0, 2)


def solution(mesh):
    placed = (P(None, "chan", None, None, "grp"), P(None, None, "chan"), P(), P(), P(), P())
    n = mesh.shape["chan"]

    def part(voltages, gains, feed_cyl, feed_ns, ew_index, ns_beam):
        fits = voltages.shape == (2, 64, 2, 2 * n, UP * DS * TOUT) and n * 64 == FEEDS
        run = functools.partial(fused, n) if fits else shards
        return run(voltages, gains, feed_cyl, feed_ns, ew_index, ns_beam)

    return jax.shard_map(
        part, mesh=mesh, in_specs=placed, out_specs=P("chan", "grp", None), check_vma=False
    )
```

```python
import functools
import math

import jax
import jax.numpy as jnp
from jax import lax
from jax.experimental import pallas as pl
from jax.experimental.pallas import tpu as pltpu
from jax.sharding import PartitionSpec as P

CYL = 4
NSF = 256
EWB = 4
NSB = 256
EW_PH = 64
UP = 16
DS = 4
FEEDS = 1024
BEAMS = 1024
TOUT = 4


eps_power = 1e-06
MESH = pl.DeviceIdType.MESH


def phase_table(feed_cyl, feed_ns, ew_index, ns_beam):
    modulus = 2 * NSF * EW_PH
    cyl_onehot = (feed_cyl[:, None] == jnp.arange(CYL, dtype=jnp.int32)[None, :]).astype(jnp.int32)
    ew_term = jnp.sum(cyl_onehot[:, None, :] * ew_index[None, :, :], axis=2)
    ns_term = feed_ns[:, None] * ns_beam[None, :] * EW_PH
    steps_int = (ew_term[:, :, None] * (2 * NSF) + ns_term[:, None, :]) % modulus
    angles = steps_int.reshape(FEEDS, EWB * NSB).astype(jnp.float32) * (2.0 * math.pi / modulus)
    cosine = jnp.cos(angles).astype(jnp.bfloat16)
    sine_part = jnp.sin(angles).astype(jnp.bfloat16)
    upper_rows = jnp.concatenate([cosine, sine_part], axis=1)
    lower_rows = jnp.concatenate([-sine_part, cosine], axis=1)
    return jnp.concatenate([upper_rows, lower_rows], axis=0)


def upchannel_table():
    bin_index = jnp.arange(UP, dtype=jnp.int32)
    angles = (bin_index[:, None] * bin_index[None, :] % UP).astype(jnp.float32) * (
        2.0 * math.pi / UP
    )
    cosine = jnp.cos(angles)
    sine_part = jnp.sin(angles)
    return jnp.stack([jnp.stack([cosine, -sine_part], -1), jnp.stack([sine_part, cosine], -1)], 1)


def shards(voltages, gains, feed_cyl, feed_ns, ew_index, ns_beam):
    weights = phase_table(feed_cyl, feed_ns, ew_index, ns_beam).reshape(2, FEEDS, 2 * BEAMS)
    fine_table = upchannel_table()
    sample = voltages.astype(jnp.float32)
    gain_real = gains[0].T[:, :, None, None]
    gain_imag = gains[1].T[:, :, None, None]
    calibrated = jnp.stack(
        [
            (gain_real * sample[0] - gain_imag * sample[1]).astype(jnp.bfloat16),
            (gain_real * sample[1] + gain_imag * sample[0]).astype(jnp.bfloat16),
        ]
    )
    arrived = lax.all_to_all(calibrated, "chan", split_axis=3, concat_axis=1, tiled=True)
    pieces = arrived.shape[2]
    channels = arrived.shape[3]
    beam_sums = jnp.einsum("rfpct,rfq->pctq", arrived, weights, preferred_element_type=jnp.float32)
    beam_sums = beam_sums.reshape(pieces, channels, TOUT, DS, UP, 2, BEAMS)
    fine_bins = jnp.einsum(
        "pcudjrb,jrks->pbudcks", beam_sums, fine_table, precision=lax.Precision.HIGHEST
    )
    beam_power = jnp.sum(jnp.sum(fine_bins * fine_bins, axis=(3, 6)), axis=0)
    total_chans = beam_power.shape[2] * lax.axis_size("chan")
    band_sum = lax.psum(jnp.sum(beam_power, axis=(2, 3)), "chan")
    baseline = band_sum / (total_chans * UP)
    normed = beam_power / (baseline[:, :, None, None] + eps_power)
    intensity = lax.all_to_all(normed, "chan", split_axis=0, concat_axis=2, tiled=True)
    return intensity.reshape(intensity.shape[0], TOUT, intensity.shape[2] * UP)

def fft(values):
    size = len(values)
    if size == 1:
        return values
    even = fft(values[0::2])
    odd = fft(values[1::2])
    low, high = [], []
    for k in range(size // 2):
        er, ei = even[k]
        xr, xi = odd[k]
        if k == 0:
            tr, ti = xr, xi
        elif 4 * k == size:
            tr, ti = xi, -xr
        else:
            c = math.cos(2.0 * math.pi * k / size)
            s = math.sin(2.0 * math.pi * k / size)
            if 8 * k == size:
                tr, ti = (xr + xi) * c, (xi - xr) * c
            elif 8 * k == 3 * size:
                tr, ti = (xi - xr) * s, -(xr + xi) * s
            else:
                tr, ti = xr * c + xi * s, xi * c - xr * s
        low.append((er + tr, ei + ti))
        high.append((er - tr, ei - ti))
    return low + high


def cos_sin(steps):
    quarter = (steps + 64) >> 7
    x = (steps - (quarter << 7)).astype(jnp.float32) * (2.0 * math.pi / 512)
    y = x * x
    s = x * (1.0 + y * (-1 / 6 + y * (1 / 120 + y * (-1 / 5040 + y * (1 / 362880)))))
    c = 1.0 + y * (-0.5 + y * (1 / 24 + y * (-1 / 720 + y * (1 / 40320))))
    odd = (quarter & 1) == 1
    cosine = jnp.where(odd, s, c)
    sine = jnp.where(odd, c, s)
    cosine = jnp.where(((quarter + 1) & 2) == 2, -cosine, cosine)
    sine = jnp.where((quarter & 2) == 2, -sine, sine)
    return cosine, sine


def beam_kernel(
    n, volt_ref, gain_ref, cyl_ref, ns_ref, ew_ref, nb_ref, out_ref,
    volt, wide, spread, gcol, ccol, ncol, xin, x_ref,
    recv, wre, wim, sums, psc, pbuf, precv, turn,
    volt_sem, send_sem, recv_sem, own_sem, psend_sem, precv_sem, pown_sem,
):
    me = lax.axis_index("chan")
    fetch = pltpu.make_async_copy(volt_ref, volt, volt_sem)
    fetch.start()
    barrier = pltpu.get_barrier_semaphore()

    def greet(s, carry):
        pl.semaphore_signal(
            barrier, inc=1, device_id={"chan": lax.rem(me + s, n)}, device_id_type=MESH
        )
        return carry

    lax.fori_loop(1, n, greet, 0)

    row = lax.broadcasted_iota(jnp.int32, spread.shape, 0)
    take = ((row >> 2) & 1) * 256 + ((row >> 7) * DS + (row & 3)) * UP + ((row >> 3) & 15)
    lane = lax.broadcasted_iota(jnp.int32, spread.shape, 1)
    spread[...] = jnp.where(take == lane, 1.0, 0.0).astype(jnp.bfloat16)
    for r in range(2):
        for p in range(2):
            gcol[r, p] = jnp.broadcast_to(gain_ref[r, p : p + 1, :], (128, 64)).T
    for i in range(FEEDS // 128):
        rows = slice(i * 128, (i + 1) * 128)
        ccol[rows, :] = jnp.broadcast_to(cyl_ref[i : i + 1, :], (128, 128)).T
        ncol[rows, :] = jnp.broadcast_to(ns_ref[i : i + 1, :], (128, 128)).T

    fetch.wait()

    def widen(i, carry):
        first = pl.multiple_of(i * 8 * 2 * n, 8 * 2 * n)
        for r in range(2):
            for p in range(2):
                part = volt[r, pl.ds(pl.multiple_of(i * 8, 8), 8), p].astype(jnp.float32)
                part = part.reshape(8 * 2 * n, 256)
                for h in range(2):
                    wide[r, p, h, pl.ds(first, 8 * 2 * n), :] = part[:, h * 128 : (h + 1) * 128]
        return carry

    lax.fori_loop(0, 8, widen, 0)
    pl.semaphore_wait(barrier, n - 1)

    mine = pl.ds(pl.multiple_of(me * 128, 128), 128)

    def volt_copy(u, s):
        d = lax.rem(me + s, n)
        return pltpu.make_async_remote_copy(
            src_ref=x_ref.at[d, u],
            dst_ref=recv.at[u, :, mine],
            send_sem=send_sem.at[u, s],
            recv_sem=recv_sem.at[u, s],
            device_id={"chan": d},
            device_id_type=MESH,
        )

    def own_copy(u):
        return pltpu.make_async_copy(x_ref.at[me, u], recv.at[u, :, mine], own_sem.at[u])

    def power_copy(u, s):
        d = lax.rem(me + s, n)
        return pltpu.make_async_remote_copy(
            src_ref=pbuf.at[u, d],
            dst_ref=precv.at[u, me],
            send_sem=psend_sem.at[u, s],
            recv_sem=precv_sem.at[u, s],
            device_id={"chan": d},
            device_id_type=MESH,
        )

    def own_power(u):
        return pltpu.make_async_copy(pbuf.at[u, me], precv.at[u, me], pown_sem.at[u])

    def each(make, act, u):
        def one(s, carry):
            getattr(make(u, s), act)()
            return carry

        lax.fori_loop(1, n, one, 0)

    def produce(i, carry):
        s = lax.rem(i + n // 2, n)
        d = lax.rem(me + s, n)
        for p in range(2):
            for c in range(2):
                for h in range(2):
                    at = pl.ds(d * 2 + c, 64, stride=2 * n)
                    real = wide[0, p, h, at, :]
                    imag = wide[1, p, h, at, :]
                    gr = gcol[0, p]
                    gi = gcol[1, p]
                    cols = slice(c * 256 + h * 128, c * 256 + h * 128 + 128)
                    xin[p * 128 : p * 128 + 64, cols] = (gr * real - gi * imag).astype(jnp.bfloat16)
                    xin[p * 128 + 64 : p * 128 + 128, cols] = (gr * imag + gi * real).astype(jnp.bfloat16)
        turned = lax.dot_general(
            spread[...], xin[...], (((1,), (1,)), ((), ())), preferred_element_type=jnp.float32
        )
        rows = jnp.concatenate(
            [turned[:, :128].reshape(TOUT * UP, 1, 8, 128), turned[:, 128:].reshape(TOUT * UP, 1, 8, 128)],
            axis=1,
        )
        x_ref[d] = rows.astype(jnp.bfloat16).reshape(TOUT, UP * 16, 128)

        @pl.when(s > 0)
        def _():
            volt_copy(0, s).start()

        return carry

    lax.fori_loop(0, n, produce, 0)
    for u in range(1, TOUT):
        each(volt_copy, "start", u)
    for u in range(TOUT):
        own_copy(u).start()

    def table(s, carry):
        feeds = pl.ds(pl.multiple_of(s * 64, 64), 64)
        top = pl.ds(pl.multiple_of(s * 128, 128), 64)
        low = pl.ds(pl.multiple_of(s * 128 + 64, 64), 64)
        cyl = ccol[feeds, :]
        for h in range(2):
            slope = ncol[feeds, :] * nb_ref[h : h + 1, :]
            for e in range(EWB):
                shift = jnp.where(
                    cyl < 2,
                    jnp.where(cyl == 0, ew_ref[e, 0], ew_ref[e, 1]),
                    jnp.where(cyl == 2, ew_ref[e, 2], ew_ref[e, 3]),
                )
                cosine, sine = cos_sin((slope + shift * 8) & 511)
                cols = slice(e * NSB + h * 128, e * NSB + h * 128 + 128)
                cosine = cosine.astype(jnp.bfloat16)
                wre[top, cols] = cosine
                wim[low, cols] = cosine
                wim[top, cols] = sine.astype(jnp.bfloat16)
                wre[low, cols] = (-sine).astype(jnp.bfloat16)
        return carry

    lax.fori_loop(0, n, table, 0)
    left = lax.broadcasted_iota(jnp.int32, (16, 128), 1) < 64

    for u in range(TOUT):
        each(volt_copy, "wait_recv", u)
        own_copy(u).wait()

        def block(nb, carry, u=u):
            cols = pl.ds(pl.multiple_of(nb * 256, 256), 256)
            sums[0] = jnp.dot(recv[u], wre[:, cols], preferred_element_type=jnp.float32)
            sums[1] = jnp.dot(recv[u], wim[:, cols], preferred_element_type=jnp.float32)
            for lane in range(2):
                at = slice(lane * 128, (lane + 1) * 128)
                total = None
                for p in range(2):
                    bins = fft(
                        [
                            (
                                sums[0, j * 16 + p * 8 : j * 16 + p * 8 + 8, at],
                                sums[1, j * 16 + p * 8 : j * 16 + p * 8 + 8, at],
                            )
                            for j in range(UP)
                        ]
                    )
                    power = [r * r + i * i for r, i in bins]
                    total = power if p == 0 else [a + b for a, b in zip(total, power)]
                for k in range(UP):
                    part = total[k]
                    part = part + pltpu.roll(part, 6, 0)
                    part = part + pltpu.roll(part, 7, 0)
                    psc[k : k + 1, :] = part[0:1]
                    psc[UP + k : UP + k + 1, :] = part[4:5]
                c0 = psc[:UP, :]
                c1 = psc[UP:, :]
                pair = (nb * 2 + lane) * 2
                pbuf[u, pair] = jnp.where(left, c0, pltpu.roll(c1, 64, 1))
                pbuf[u, pair + 1] = jnp.where(left, pltpu.roll(c0, 64, 1), c1)
            return carry

        lax.fori_loop(0, BEAMS // 256, block, 0)
        each(power_copy, "start", u)
        own_power(u).start()

    for u in range(TOUT):
        each(volt_copy, "wait_send", u)

    for u in range(TOUT):
        each(power_copy, "wait_recv", u)
        own_power(u).wait()

        def gather(src, carry, u=u):
            rows = precv[u, src]
            first = pl.multiple_of(src * 32, 32)
            turn[pl.ds(first, 16), :] = rows
            turn[pl.ds(first + 16, 16), :] = pltpu.roll(rows, 64, 1)
            return carry

        lax.fori_loop(0, n, gather, 0)
        beams = jnp.concatenate(
            [turn[i * 128 : (i + 1) * 128, :].T[:64] for i in range(n * 32 // 128)], axis=1
        )
        baseline = jnp.sum(beams, axis=1, keepdims=True) / (n * 32)
        out_ref[u] = beams / (baseline + eps_power)
    for u in range(TOUT):
        each(power_copy, "wait_send", u)


def fused(n, voltages, gains, feed_cyl, feed_ns, ew_index, ns_beam):
    vmem = pl.BlockSpec(memory_space=pltpu.VMEM)
    dma = pltpu.SemaphoreType.DMA
    out = pl.pallas_call(
        functools.partial(beam_kernel, n),
        out_shape=jax.ShapeDtypeStruct((TOUT, BEAMS // n, n * 32), jnp.float32),
        in_specs=[
            pl.BlockSpec(memory_space=pl.ANY), vmem, vmem, vmem,
            pl.BlockSpec(memory_space=pltpu.SMEM), vmem,
        ],
        out_specs=vmem,
        scratch_shapes=[
            pltpu.VMEM(voltages.shape, jnp.bfloat16),
            pltpu.VMEM((2, 2, 2, 64 * 2 * n, 128), jnp.float32),
            pltpu.VMEM((512, 512), jnp.bfloat16),
            pltpu.VMEM((2, 2, 64, 128), jnp.float32),
            pltpu.VMEM((FEEDS, 128), jnp.int32),
            pltpu.VMEM((FEEDS, 128), jnp.int32),
            pltpu.VMEM((256, 512), jnp.bfloat16),
            pltpu.VMEM((n, TOUT, 256, 128), jnp.bfloat16),
            pltpu.VMEM((TOUT, 256, n * 128), jnp.bfloat16),
            pltpu.VMEM((2 * FEEDS, BEAMS), jnp.bfloat16),
            pltpu.VMEM((2 * FEEDS, BEAMS), jnp.bfloat16),
            pltpu.VMEM((2, 256, 256), jnp.float32),
            pltpu.VMEM((2 * UP, 128), jnp.float32),
            pltpu.VMEM((TOUT, n, 16, 128), jnp.float32),
            pltpu.VMEM((TOUT, n, 16, 128), jnp.float32),
            pltpu.VMEM((n * 32, 128), jnp.float32),
            dma, dma((TOUT, n)), dma((TOUT, n)), dma((TOUT,)),
            dma((TOUT, n)), dma((TOUT, n)), dma((TOUT,)),
        ],
        compiler_params=pltpu.CompilerParams(
            collective_id=0, has_side_effects=True, vmem_limit_bytes=56 << 20
        ),
    )(
        voltages, gains, feed_cyl.reshape(-1, 128), feed_ns.reshape(-1, 128),
        ew_index, ns_beam.reshape(-1, 128),
    )
    return out.transpose(1, 0, 2)


def solution(mesh):
    placed = (P(None, "chan", None, None, "grp"), P(None, None, "chan"), P(), P(), P(), P())
    n = mesh.shape["chan"]

    def part(voltages, gains, feed_cyl, feed_ns, ew_index, ns_beam):
        fits = voltages.shape == (2, 64, 2, 2 * n, UP * DS * TOUT) and n * 64 == FEEDS
        run = functools.partial(fused, n) if fits else shards
        return run(voltages, gains, feed_cyl, feed_ns, ew_index, ns_beam)

    return jax.shard_map(
        part, mesh=mesh, in_specs=placed, out_specs=P("chan", "grp", None), check_vma=False
    )
```

```python
import functools
import math

import jax
import jax.numpy as jnp
from jax import lax
from jax.experimental import pallas as pl
from jax.experimental.pallas import tpu as pltpu
from jax.sharding import PartitionSpec as P

CYL = 4
NSF = 256
EWB = 4
NSB = 256
EW_PH = 64
UP = 16
DS = 4
FEEDS = 1024
BEAMS = 1024
TOUT = 4


eps_power = 1e-06
MESH = pl.DeviceIdType.MESH


def phase_table(feed_cyl, feed_ns, ew_index, ns_beam):
    modulus = 2 * NSF * EW_PH
    cyl_onehot = (feed_cyl[:, None] == jnp.arange(CYL, dtype=jnp.int32)[None, :]).astype(jnp.int32)
    ew_term = jnp.sum(cyl_onehot[:, None, :] * ew_index[None, :, :], axis=2)
    ns_term = feed_ns[:, None] * ns_beam[None, :] * EW_PH
    steps_int = (ew_term[:, :, None] * (2 * NSF) + ns_term[:, None, :]) % modulus
    angles = steps_int.reshape(FEEDS, EWB * NSB).astype(jnp.float32) * (2.0 * math.pi / modulus)
    cosine = jnp.cos(angles).astype(jnp.bfloat16)
    sine_part = jnp.sin(angles).astype(jnp.bfloat16)
    upper_rows = jnp.concatenate([cosine, sine_part], axis=1)
    lower_rows = jnp.concatenate([-sine_part, cosine], axis=1)
    return jnp.concatenate([upper_rows, lower_rows], axis=0)


def upchannel_table():
    bin_index = jnp.arange(UP, dtype=jnp.int32)
    angles = (bin_index[:, None] * bin_index[None, :] % UP).astype(jnp.float32) * (
        2.0 * math.pi / UP
    )
    cosine = jnp.cos(angles)
    sine_part = jnp.sin(angles)
    return jnp.stack([jnp.stack([cosine, -sine_part], -1), jnp.stack([sine_part, cosine], -1)], 1)


def shards(voltages, gains, feed_cyl, feed_ns, ew_index, ns_beam):
    weights = phase_table(feed_cyl, feed_ns, ew_index, ns_beam).reshape(2, FEEDS, 2 * BEAMS)
    fine_table = upchannel_table()
    sample = voltages.astype(jnp.float32)
    gain_real = gains[0].T[:, :, None, None]
    gain_imag = gains[1].T[:, :, None, None]
    calibrated = jnp.stack(
        [
            (gain_real * sample[0] - gain_imag * sample[1]).astype(jnp.bfloat16),
            (gain_real * sample[1] + gain_imag * sample[0]).astype(jnp.bfloat16),
        ]
    )
    arrived = lax.all_to_all(calibrated, "chan", split_axis=3, concat_axis=1, tiled=True)
    pieces = arrived.shape[2]
    channels = arrived.shape[3]
    beam_sums = jnp.einsum("rfpct,rfq->pctq", arrived, weights, preferred_element_type=jnp.float32)
    beam_sums = beam_sums.reshape(pieces, channels, TOUT, DS, UP, 2, BEAMS)
    fine_bins = jnp.einsum(
        "pcudjrb,jrks->pbudcks", beam_sums, fine_table, precision=lax.Precision.HIGHEST
    )
    beam_power = jnp.sum(jnp.sum(fine_bins * fine_bins, axis=(3, 6)), axis=0)
    total_chans = beam_power.shape[2] * lax.axis_size("chan")
    band_sum = lax.psum(jnp.sum(beam_power, axis=(2, 3)), "chan")
    baseline = band_sum / (total_chans * UP)
    normed = beam_power / (baseline[:, :, None, None] + eps_power)
    intensity = lax.all_to_all(normed, "chan", split_axis=0, concat_axis=2, tiled=True)
    return intensity.reshape(intensity.shape[0], TOUT, intensity.shape[2] * UP)

def fft(values):
    size = len(values)
    if size == 1:
        return values
    even = fft(values[0::2])
    odd = fft(values[1::2])
    low, high = [], []
    for k in range(size // 2):
        er, ei = even[k]
        xr, xi = odd[k]
        if k == 0:
            tr, ti = xr, xi
        elif 4 * k == size:
            tr, ti = xi, -xr
        else:
            c = math.cos(2.0 * math.pi * k / size)
            s = math.sin(2.0 * math.pi * k / size)
            if 8 * k == size:
                tr, ti = (xr + xi) * c, (xi - xr) * c
            elif 8 * k == 3 * size:
                tr, ti = (xi - xr) * s, -(xr + xi) * s
            else:
                tr, ti = xr * c + xi * s, xi * c - xr * s
        low.append((er + tr, ei + ti))
        high.append((er - tr, ei - ti))
    return low + high


def cos_sin(steps):
    quarter = (steps + 64) >> 7
    x = (steps - (quarter << 7)).astype(jnp.float32) * (2.0 * math.pi / 512)
    y = x * x
    s = x * (1.0 + y * (-1 / 6 + y * (1 / 120 + y * (-1 / 5040 + y * (1 / 362880)))))
    c = 1.0 + y * (-0.5 + y * (1 / 24 + y * (-1 / 720 + y * (1 / 40320))))
    odd = (quarter & 1) == 1
    cosine = jnp.where(odd, s, c)
    sine = jnp.where(odd, c, s)
    cosine = jnp.where(((quarter + 1) & 2) == 2, -cosine, cosine)
    sine = jnp.where((quarter & 2) == 2, -sine, sine)
    return cosine, sine


def beam_kernel(
    n, volt_ref, gain_ref, cyl_ref, ns_ref, ew_ref, nb_ref, out_ref,
    volt, wide, spread, gcol, ccol, ncol, xin, x_ref,
    recv, wre, wim, sums, psc, pbuf, precv, turn,
    volt_sem, send_sem, recv_sem, own_sem, psend_sem, precv_sem, pown_sem,
):
    me = lax.axis_index("chan")

    def fetch(i):
        feeds = pl.ds(pl.multiple_of(i * 8, 8), 8)
        return pltpu.make_async_copy(volt_ref.at[:, feeds], volt.at[:, feeds], volt_sem.at[i])

    def begin(i, carry):
        fetch(i).start()
        return carry

    lax.fori_loop(0, 8, begin, 0)
    barrier = pltpu.get_barrier_semaphore()

    def greet(s, carry):
        pl.semaphore_signal(
            barrier, inc=1, device_id={"chan": lax.rem(me + s, n)}, device_id_type=MESH
        )
        return carry

    lax.fori_loop(1, n, greet, 0)

    row = lax.broadcasted_iota(jnp.int32, spread.shape, 0)
    take = ((row >> 2) & 1) * 256 + ((row >> 7) * DS + (row & 3)) * UP + ((row >> 3) & 15)
    lane = lax.broadcasted_iota(jnp.int32, spread.shape, 1)
    spread[...] = jnp.where(take == lane, 1.0, 0.0).astype(jnp.bfloat16)
    for r in range(2):
        for p in range(2):
            gcol[r, p] = jnp.broadcast_to(gain_ref[r, p : p + 1, :], (128, 64)).T
    def widen(i, carry):
        fetch(i).wait()
        first = pl.multiple_of(i * 8 * 2 * n, 8 * 2 * n)
        for r in range(2):
            for p in range(2):
                part = volt[r, pl.ds(pl.multiple_of(i * 8, 8), 8), p].astype(jnp.float32)
                part = part.reshape(8 * 2 * n, 256)
                for h in range(2):
                    wide[r, p, h, pl.ds(first, 8 * 2 * n), :] = part[:, h * 128 : (h + 1) * 128]
        return carry

    lax.fori_loop(0, 8, widen, 0)
    pl.semaphore_wait(barrier, n - 1)

    mine = pl.ds(pl.multiple_of(me * 128, 128), 128)

    def volt_copy(u, s):
        d = lax.rem(me + s, n)
        return pltpu.make_async_remote_copy(
            src_ref=x_ref.at[d, u],
            dst_ref=recv.at[u, :, mine],
            send_sem=send_sem.at[u, s],
            recv_sem=recv_sem.at[u, s],
            device_id={"chan": d},
            device_id_type=MESH,
        )

    def own_copy(u):
        return pltpu.make_async_copy(x_ref.at[me, u], recv.at[u, :, mine], own_sem.at[u])

    def power_copy(u, s):
        d = lax.rem(me + s, n)
        return pltpu.make_async_remote_copy(
            src_ref=pbuf.at[u, d],
            dst_ref=precv.at[u, me],
            send_sem=psend_sem.at[u, s],
            recv_sem=precv_sem.at[u, s],
            device_id={"chan": d},
            device_id_type=MESH,
        )

    def own_power(u):
        return pltpu.make_async_copy(pbuf.at[u, me], precv.at[u, me], pown_sem.at[u])

    def each(make, act, u):
        def one(s, carry):
            getattr(make(u, s), act)()
            return carry

        lax.fori_loop(1, n, one, 0)

    def produce(i, carry):
        s = lax.rem(i + n // 2, n)
        d = lax.rem(me + s, n)
        for p in range(2):
            for c in range(2):
                for h in range(2):
                    at = pl.ds(d * 2 + c, 64, stride=2 * n)
                    real = wide[0, p, h, at, :]
                    imag = wide[1, p, h, at, :]
                    gr = gcol[0, p]
                    gi = gcol[1, p]
                    cols = slice(c * 256 + h * 128, c * 256 + h * 128 + 128)
                    xin[p * 128 : p * 128 + 64, cols] = (gr * real - gi * imag).astype(jnp.bfloat16)
                    xin[p * 128 + 64 : p * 128 + 128, cols] = (gr * imag + gi * real).astype(jnp.bfloat16)
        turned = lax.dot_general(
            spread[...], xin[...], (((1,), (1,)), ((), ())), preferred_element_type=jnp.float32
        )
        rows = jnp.concatenate(
            [turned[:, :128].reshape(TOUT * UP, 1, 8, 128), turned[:, 128:].reshape(TOUT * UP, 1, 8, 128)],
            axis=1,
        )
        x_ref[d] = rows.astype(jnp.bfloat16).reshape(TOUT, UP * 16, 128)

        @pl.when(s > 0)
        def _():
            volt_copy(0, s).start()

        return carry

    lax.fori_loop(0, n, produce, 0)
    for u in range(1, TOUT):
        each(volt_copy, "start", u)
    for u in range(TOUT):
        own_copy(u).start()

    for i in range(FEEDS // 128):
        rows = slice(i * 128, (i + 1) * 128)
        ccol[rows, :] = jnp.broadcast_to(cyl_ref[i : i + 1, :], (128, 128)).T
        ncol[rows, :] = jnp.broadcast_to(ns_ref[i : i + 1, :], (128, 128)).T

    def table(s, carry):
        feeds = pl.ds(pl.multiple_of(s * 64, 64), 64)
        top = pl.ds(pl.multiple_of(s * 128, 128), 64)
        low = pl.ds(pl.multiple_of(s * 128 + 64, 64), 64)
        cyl = ccol[feeds, :]
        for h in range(2):
            slope = ncol[feeds, :] * nb_ref[h : h + 1, :]
            for e in range(EWB):
                shift = jnp.where(
                    cyl < 2,
                    jnp.where(cyl == 0, ew_ref[e, 0], ew_ref[e, 1]),
                    jnp.where(cyl == 2, ew_ref[e, 2], ew_ref[e, 3]),
                )
                cosine, sine = cos_sin((slope + shift * 8) & 511)
                cols = slice(e * NSB + h * 128, e * NSB + h * 128 + 128)
                cosine = cosine.astype(jnp.bfloat16)
                wre[top, cols] = cosine
                wim[low, cols] = cosine
                wim[top, cols] = sine.astype(jnp.bfloat16)
                wre[low, cols] = (-sine).astype(jnp.bfloat16)
        return carry

    lax.fori_loop(0, n, table, 0)
    blocks = BEAMS // 256
    left = lax.broadcasted_iota(jnp.int32, (16, 128), 1) < 64

    for u in range(TOUT):
        each(volt_copy, "wait_recv", u)
        own_copy(u).wait()

        def block(i, carry, u=u):
            nb = lax.rem(i + me * blocks // n + blocks // 2, blocks)
            cols = pl.ds(pl.multiple_of(nb * 256, 256), 256)
            sums[0] = jnp.dot(recv[u], wre[:, cols], preferred_element_type=jnp.float32)
            sums[1] = jnp.dot(recv[u], wim[:, cols], preferred_element_type=jnp.float32)
            for lane in range(2):
                at = slice(lane * 128, (lane + 1) * 128)
                total = None
                for p in range(2):
                    bins = fft(
                        [
                            (
                                sums[0, j * 16 + p * 8 : j * 16 + p * 8 + 8, at],
                                sums[1, j * 16 + p * 8 : j * 16 + p * 8 + 8, at],
                            )
                            for j in range(UP)
                        ]
                    )
                    power = [r * r + i * i for r, i in bins]
                    total = power if p == 0 else [a + b for a, b in zip(total, power)]
                for k in range(UP):
                    part = total[k]
                    part = part + pltpu.roll(part, 6, 0)
                    part = part + pltpu.roll(part, 7, 0)
                    psc[k : k + 1, :] = part[0:1]
                    psc[UP + k : UP + k + 1, :] = part[4:5]
                c0 = psc[:UP, :]
                c1 = psc[UP:, :]
                pair = (nb * 2 + lane) * 2
                pbuf[u, pair] = jnp.where(left, c0, pltpu.roll(c1, 64, 1))
                pbuf[u, pair + 1] = jnp.where(left, pltpu.roll(c0, 64, 1), c1)
            for q in range(n // blocks):
                s = lax.rem(nb * (n // blocks) + q - me + n, n)

                @pl.when(s > 0)
                def _(s=s):
                    power_copy(u, s).start()

            return carry

        lax.fori_loop(0, blocks, block, 0)
        own_power(u).start()

    for u in range(TOUT):
        each(volt_copy, "wait_send", u)

    for u in range(TOUT):
        each(power_copy, "wait_recv", u)
        own_power(u).wait()

        def gather(src, carry, u=u):
            rows = precv[u, src]
            first = pl.multiple_of(src * 32, 32)
            turn[pl.ds(first, 16), :] = rows
            turn[pl.ds(first + 16, 16), :] = pltpu.roll(rows, 64, 1)
            return carry

        lax.fori_loop(0, n, gather, 0)
        beams = jnp.concatenate(
            [turn[i * 128 : (i + 1) * 128, :].T[:64] for i in range(n * 32 // 128)], axis=1
        )
        baseline = jnp.sum(beams, axis=1, keepdims=True) / (n * 32)
        out_ref[u] = beams / (baseline + eps_power)
    for u in range(TOUT):
        each(power_copy, "wait_send", u)


def fused(n, voltages, gains, feed_cyl, feed_ns, ew_index, ns_beam):
    vmem = pl.BlockSpec(memory_space=pltpu.VMEM)
    dma = pltpu.SemaphoreType.DMA
    out = pl.pallas_call(
        functools.partial(beam_kernel, n),
        out_shape=jax.ShapeDtypeStruct((TOUT, BEAMS // n, n * 32), jnp.float32),
        in_specs=[
            pl.BlockSpec(memory_space=pltpu.HBM), vmem, vmem, vmem,
            pl.BlockSpec(memory_space=pltpu.SMEM), vmem,
        ],
        out_specs=vmem,
        scratch_shapes=[
            pltpu.VMEM(voltages.shape, jnp.bfloat16),
            pltpu.VMEM((2, 2, 2, 64 * 2 * n, 128), jnp.float32),
            pltpu.VMEM((512, 512), jnp.bfloat16),
            pltpu.VMEM((2, 2, 64, 128), jnp.float32),
            pltpu.VMEM((FEEDS, 128), jnp.int32),
            pltpu.VMEM((FEEDS, 128), jnp.int32),
            pltpu.VMEM((256, 512), jnp.bfloat16),
            pltpu.VMEM((n, TOUT, 256, 128), jnp.bfloat16),
            pltpu.VMEM((TOUT, 256, n * 128), jnp.bfloat16),
            pltpu.VMEM((2 * FEEDS, BEAMS), jnp.bfloat16),
            pltpu.VMEM((2 * FEEDS, BEAMS), jnp.bfloat16),
            pltpu.VMEM((2, 256, 256), jnp.float32),
            pltpu.VMEM((2 * UP, 128), jnp.float32),
            pltpu.VMEM((TOUT, n, 16, 128), jnp.float32),
            pltpu.VMEM((TOUT, n, 16, 128), jnp.float32),
            pltpu.VMEM((n * 32, 128), jnp.float32),
            dma((8,)), dma((TOUT, n)), dma((TOUT, n)), dma((TOUT,)),
            dma((TOUT, n)), dma((TOUT, n)), dma((TOUT,)),
        ],
        compiler_params=pltpu.CompilerParams(
            collective_id=0, has_side_effects=True, vmem_limit_bytes=40 << 20
        ),
    )(
        voltages, gains, feed_cyl.reshape(-1, 128), feed_ns.reshape(-1, 128),
        ew_index, ns_beam.reshape(-1, 128),
    )
    return out.transpose(1, 0, 2)


def solution(mesh):
    placed = (P(None, "chan", None, None, "grp"), P(None, None, "chan"), P(), P(), P(), P())
    n = mesh.shape["chan"]

    def part(voltages, gains, feed_cyl, feed_ns, ew_index, ns_beam):
        fits = voltages.shape == (2, 64, 2, 2 * n, UP * DS * TOUT) and n * 64 == FEEDS
        run = functools.partial(fused, n) if fits else shards
        return run(voltages, gains, feed_cyl, feed_ns, ew_index, ns_beam)

    return jax.shard_map(
        part, mesh=mesh, in_specs=placed, out_specs=P("chan", "grp", None), check_vma=False
    )
```

```python
import functools
import math

import jax
import jax.numpy as jnp
from jax import lax
from jax.experimental import pallas as pl
from jax.experimental.pallas import tpu as pltpu
from jax.sharding import PartitionSpec as P

CYL = 4
NSF = 256
EWB = 4
NSB = 256
EW_PH = 64
UP = 16
DS = 4
FEEDS = 1024
BEAMS = 1024
TOUT = 4


eps_power = 1e-06
MESH = pl.DeviceIdType.MESH


def phase_table(feed_cyl, feed_ns, ew_index, ns_beam):
    modulus = 2 * NSF * EW_PH
    cyl_onehot = (feed_cyl[:, None] == jnp.arange(CYL, dtype=jnp.int32)[None, :]).astype(jnp.int32)
    ew_term = jnp.sum(cyl_onehot[:, None, :] * ew_index[None, :, :], axis=2)
    ns_term = feed_ns[:, None] * ns_beam[None, :] * EW_PH
    steps_int = (ew_term[:, :, None] * (2 * NSF) + ns_term[:, None, :]) % modulus
    angles = steps_int.reshape(FEEDS, EWB * NSB).astype(jnp.float32) * (2.0 * math.pi / modulus)
    cosine = jnp.cos(angles).astype(jnp.bfloat16)
    sine_part = jnp.sin(angles).astype(jnp.bfloat16)
    upper_rows = jnp.concatenate([cosine, sine_part], axis=1)
    lower_rows = jnp.concatenate([-sine_part, cosine], axis=1)
    return jnp.concatenate([upper_rows, lower_rows], axis=0)


def upchannel_table():
    bin_index = jnp.arange(UP, dtype=jnp.int32)
    angles = (bin_index[:, None] * bin_index[None, :] % UP).astype(jnp.float32) * (
        2.0 * math.pi / UP
    )
    cosine = jnp.cos(angles)
    sine_part = jnp.sin(angles)
    return jnp.stack([jnp.stack([cosine, -sine_part], -1), jnp.stack([sine_part, cosine], -1)], 1)


def shards(voltages, gains, feed_cyl, feed_ns, ew_index, ns_beam):
    weights = phase_table(feed_cyl, feed_ns, ew_index, ns_beam).reshape(2, FEEDS, 2 * BEAMS)
    fine_table = upchannel_table()
    sample = voltages.astype(jnp.float32)
    gain_real = gains[0].T[:, :, None, None]
    gain_imag = gains[1].T[:, :, None, None]
    calibrated = jnp.stack(
        [
            (gain_real * sample[0] - gain_imag * sample[1]).astype(jnp.bfloat16),
            (gain_real * sample[1] + gain_imag * sample[0]).astype(jnp.bfloat16),
        ]
    )
    arrived = lax.all_to_all(calibrated, "chan", split_axis=3, concat_axis=1, tiled=True)
    pieces = arrived.shape[2]
    channels = arrived.shape[3]
    beam_sums = jnp.einsum("rfpct,rfq->pctq", arrived, weights, preferred_element_type=jnp.float32)
    beam_sums = beam_sums.reshape(pieces, channels, TOUT, DS, UP, 2, BEAMS)
    fine_bins = jnp.einsum(
        "pcudjrb,jrks->pbudcks", beam_sums, fine_table, precision=lax.Precision.HIGHEST
    )
    beam_power = jnp.sum(jnp.sum(fine_bins * fine_bins, axis=(3, 6)), axis=0)
    total_chans = beam_power.shape[2] * lax.axis_size("chan")
    band_sum = lax.psum(jnp.sum(beam_power, axis=(2, 3)), "chan")
    baseline = band_sum / (total_chans * UP)
    normed = beam_power / (baseline[:, :, None, None] + eps_power)
    intensity = lax.all_to_all(normed, "chan", split_axis=0, concat_axis=2, tiled=True)
    return intensity.reshape(intensity.shape[0], TOUT, intensity.shape[2] * UP)

def fft(values):
    size = len(values)
    if size == 1:
        return values
    even = fft(values[0::2])
    odd = fft(values[1::2])
    low, high = [], []
    for k in range(size // 2):
        er, ei = even[k]
        xr, xi = odd[k]
        if k == 0:
            tr, ti = xr, xi
        elif 4 * k == size:
            tr, ti = xi, -xr
        else:
            c = math.cos(2.0 * math.pi * k / size)
            s = math.sin(2.0 * math.pi * k / size)
            if 8 * k == size:
                tr, ti = (xr + xi) * c, (xi - xr) * c
            elif 8 * k == 3 * size:
                tr, ti = (xi - xr) * s, -(xr + xi) * s
            else:
                tr, ti = xr * c + xi * s, xi * c - xr * s
        low.append((er + tr, ei + ti))
        high.append((er - tr, ei - ti))
    return low + high


def cos_sin(steps):
    quarter = (steps + 64) >> 7
    x = (steps - (quarter << 7)).astype(jnp.float32) * (2.0 * math.pi / 512)
    y = x * x
    s = x * (1.0 + y * (-1 / 6 + y * (1 / 120 + y * (-1 / 5040 + y * (1 / 362880)))))
    c = 1.0 + y * (-0.5 + y * (1 / 24 + y * (-1 / 720 + y * (1 / 40320))))
    odd = (quarter & 1) == 1
    cosine = jnp.where(odd, s, c)
    sine = jnp.where(odd, c, s)
    cosine = jnp.where(((quarter + 1) & 2) == 2, -cosine, cosine)
    sine = jnp.where((quarter & 2) == 2, -sine, sine)
    return cosine, sine


def beam_kernel(
    n, volt_ref, gain_ref, cyl_ref, ns_ref, ew_ref, nb_ref, out_ref,
    volt, wide, spread, gcol, ccol, ncol, xin, x_ref,
    recv, wre, wim, sums, psc, pbuf, precv, turn,
    volt_sem, send_sem, recv_sem, own_sem, psend_sem, precv_sem, pown_sem,
):
    me = lax.axis_index("chan")

    def fetch(i):
        feeds = pl.ds(pl.multiple_of(i * 8, 8), 8)
        return pltpu.make_async_copy(volt_ref.at[:, feeds], volt.at[:, feeds], volt_sem.at[i])

    def begin(i, carry):
        fetch(i).start()
        return carry

    lax.fori_loop(0, 8, begin, 0)
    barrier = pltpu.get_barrier_semaphore()

    def greet(s, carry):
        pl.semaphore_signal(
            barrier, inc=1, device_id={"chan": lax.rem(me + s, n)}, device_id_type=MESH
        )
        return carry

    lax.fori_loop(1, n, greet, 0)

    row = lax.broadcasted_iota(jnp.int32, spread.shape, 0)
    take = ((row >> 2) & 1) * 256 + ((row >> 7) * DS + (row & 3)) * UP + ((row >> 3) & 15)
    lane = lax.broadcasted_iota(jnp.int32, spread.shape, 1)
    spread[...] = jnp.where(take == lane, 1.0, 0.0).astype(jnp.bfloat16)
    for r in range(2):
        for p in range(2):
            gcol[r, p] = jnp.broadcast_to(gain_ref[r, p : p + 1, :], (128, 64)).T
    def widen(i, carry):
        fetch(i).wait()
        first = pl.multiple_of(i * 8 * 2 * n, 8 * 2 * n)
        for r in range(2):
            for p in range(2):
                part = volt[r, pl.ds(pl.multiple_of(i * 8, 8), 8), p].astype(jnp.float32)
                part = part.reshape(8 * 2 * n, 256)
                for h in range(2):
                    wide[r, p, h, pl.ds(first, 8 * 2 * n), :] = part[:, h * 128 : (h + 1) * 128]
        return carry

    lax.fori_loop(0, 8, widen, 0)
    pl.semaphore_wait(barrier, n - 1)

    mine = pl.ds(pl.multiple_of(me * 128, 128), 128)

    def volt_copy(u, s):
        d = lax.rem(me + s, n)
        return pltpu.make_async_remote_copy(
            src_ref=x_ref.at[d, u],
            dst_ref=recv.at[u, :, mine],
            send_sem=send_sem.at[u, s],
            recv_sem=recv_sem.at[u, s],
            device_id={"chan": d},
            device_id_type=MESH,
        )

    def own_copy(u):
        return pltpu.make_async_copy(x_ref.at[me, u], recv.at[u, :, mine], own_sem.at[u])

    def power_copy(u, s):
        d = lax.rem(me + s, n)
        return pltpu.make_async_remote_copy(
            src_ref=pbuf.at[u, d],
            dst_ref=precv.at[u, me],
            send_sem=psend_sem.at[u, s],
            recv_sem=precv_sem.at[u, s],
            device_id={"chan": d},
            device_id_type=MESH,
        )

    def own_power(u):
        return pltpu.make_async_copy(pbuf.at[u, me], precv.at[u, me], pown_sem.at[u])

    def each(make, act, u):
        def one(s, carry):
            getattr(make(u, s), act)()
            return carry

        lax.fori_loop(1, n, one, 0)

    def produce(i, carry):
        s = lax.rem(i + n // 2, n)
        d = lax.rem(me + s, n)
        for p in range(2):
            for c in range(2):
                for h in range(2):
                    at = pl.ds(d * 2 + c, 64, stride=2 * n)
                    real = wide[0, p, h, at, :]
                    imag = wide[1, p, h, at, :]
                    gr = gcol[0, p]
                    gi = gcol[1, p]
                    cols = slice(c * 256 + h * 128, c * 256 + h * 128 + 128)
                    xin[p * 128 : p * 128 + 64, cols] = (gr * real - gi * imag).astype(jnp.bfloat16)
                    xin[p * 128 + 64 : p * 128 + 128, cols] = (gr * imag + gi * real).astype(jnp.bfloat16)
        turned = lax.dot_general(
            spread[...], xin[...], (((1,), (1,)), ((), ())), preferred_element_type=jnp.float32
        )
        rows = jnp.concatenate(
            [turned[:, :128].reshape(TOUT * UP, 1, 8, 128), turned[:, 128:].reshape(TOUT * UP, 1, 8, 128)],
            axis=1,
        )
        x_ref[d] = rows.astype(jnp.bfloat16).reshape(TOUT, UP * 16, 128)

        @pl.when(s > 0)
        def _():
            volt_copy(0, s).start()

        return carry

    lax.fori_loop(0, n, produce, 0)
    for u in range(1, TOUT):
        each(volt_copy, "start", u)
    for u in range(TOUT):
        own_copy(u).start()

    for i in range(FEEDS // 128):
        rows = slice(i * 128, (i + 1) * 128)
        ccol[rows, :] = jnp.broadcast_to(cyl_ref[i : i + 1, :], (128, 128)).T
        ncol[rows, :] = jnp.broadcast_to(ns_ref[i : i + 1, :], (128, 128)).T

    def table(s, carry):
        feeds = pl.ds(pl.multiple_of(s * 64, 64), 64)
        top = pl.ds(pl.multiple_of(s * 128, 128), 64)
        low = pl.ds(pl.multiple_of(s * 128 + 64, 64), 64)
        cyl = ccol[feeds, :]
        for h in range(2):
            slope = ncol[feeds, :] * nb_ref[h : h + 1, :]
            for e in range(EWB):
                shift = jnp.where(
                    cyl < 2,
                    jnp.where(cyl == 0, ew_ref[e, 0], ew_ref[e, 1]),
                    jnp.where(cyl == 2, ew_ref[e, 2], ew_ref[e, 3]),
                )
                cosine, sine = cos_sin((slope + shift * 8) & 511)
                cols = slice(e * NSB + h * 128, e * NSB + h * 128 + 128)
                cosine = cosine.astype(jnp.bfloat16)
                wre[top, cols] = cosine
                wim[low, cols] = cosine
                wim[top, cols] = sine.astype(jnp.bfloat16)
                wre[low, cols] = (-sine).astype(jnp.bfloat16)
        return carry

    lax.fori_loop(0, n, table, 0)
    blocks = BEAMS // 256
    left = lax.broadcasted_iota(jnp.int32, (16, 128), 1) < 64

    for u in range(TOUT):
        each(volt_copy, "wait_recv", u)
        own_copy(u).wait()

        def block(i, carry, u=u):
            nb = lax.rem(i + me * blocks // n + blocks // 2, blocks)
            cols = pl.ds(pl.multiple_of(nb * 256, 256), 256)
            sums[0] = jnp.dot(recv[u], wre[:, cols], preferred_element_type=jnp.float32)
            sums[1] = jnp.dot(recv[u], wim[:, cols], preferred_element_type=jnp.float32)
            for lane in range(2):
                at = slice(lane * 128, (lane + 1) * 128)
                total = None
                for p in range(2):
                    bins = fft(
                        [
                            (
                                sums[0, j * 16 + p * 8 : j * 16 + p * 8 + 8, at],
                                sums[1, j * 16 + p * 8 : j * 16 + p * 8 + 8, at],
                            )
                            for j in range(UP)
                        ]
                    )
                    power = [r * r + i * i for r, i in bins]
                    total = power if p == 0 else [a + b for a, b in zip(total, power)]
                for k in range(UP):
                    part = total[k]
                    part = part + pltpu.roll(part, 6, 0)
                    part = part + pltpu.roll(part, 7, 0)
                    psc[k : k + 1, :] = part[0:1]
                    psc[UP + k : UP + k + 1, :] = part[4:5]
                c0 = psc[:UP, :]
                c1 = psc[UP:, :]
                pair = (nb * 2 + lane) * 2
                pbuf[u, pair] = jnp.where(left, c0, pltpu.roll(c1, 64, 1))
                pbuf[u, pair + 1] = jnp.where(left, pltpu.roll(c0, 64, 1), c1)
            for q in range(n // blocks):
                s = lax.rem(nb * (n // blocks) + q - me + n, n)

                @pl.when(s > 0)
                def _(s=s):
                    power_copy(u, s).start()

            return carry

        lax.fori_loop(0, blocks, block, 0)
        own_power(u).start()

    for u in range(TOUT):
        each(volt_copy, "wait_send", u)

    for u in range(TOUT):
        each(power_copy, "wait_recv", u)
        own_power(u).wait()

        def gather(src, carry, u=u):
            rows = precv[u, src]
            first = pl.multiple_of(src * 32, 32)
            turn[pl.ds(first, 16), :] = rows
            turn[pl.ds(first + 16, 16), :] = pltpu.roll(rows, 64, 1)
            return carry

        lax.fori_loop(0, n, gather, 0)
        beams = jnp.concatenate(
            [turn[i * 128 : (i + 1) * 128, :].T[:64] for i in range(n * 32 // 128)], axis=1
        )
        baseline = jnp.sum(beams, axis=1, keepdims=True) / (n * 32)
        out_ref[u] = beams / (baseline + eps_power)
    for u in range(TOUT):
        each(power_copy, "wait_send", u)


def fused(n, voltages, gains, feed_cyl, feed_ns, ew_index, ns_beam):
    vmem = pl.BlockSpec(memory_space=pltpu.VMEM)
    dma = pltpu.SemaphoreType.DMA
    out = pl.pallas_call(
        functools.partial(beam_kernel, n),
        out_shape=jax.ShapeDtypeStruct((TOUT, BEAMS // n, n * 32), jnp.float32),
        in_specs=[
            pl.BlockSpec(memory_space=pl.ANY), vmem, vmem, vmem,
            pl.BlockSpec(memory_space=pltpu.SMEM), vmem,
        ],
        out_specs=vmem,
        scratch_shapes=[
            pltpu.VMEM(voltages.shape, jnp.bfloat16),
            pltpu.VMEM((2, 2, 2, 64 * 2 * n, 128), jnp.float32),
            pltpu.VMEM((512, 512), jnp.bfloat16),
            pltpu.VMEM((2, 2, 64, 128), jnp.float32),
            pltpu.VMEM((FEEDS, 128), jnp.int32),
            pltpu.VMEM((FEEDS, 128), jnp.int32),
            pltpu.VMEM((256, 512), jnp.bfloat16),
            pltpu.VMEM((n, TOUT, 256, 128), jnp.bfloat16),
            pltpu.VMEM((TOUT, 256, n * 128), jnp.bfloat16),
            pltpu.VMEM((2 * FEEDS, BEAMS), jnp.bfloat16),
            pltpu.VMEM((2 * FEEDS, BEAMS), jnp.bfloat16),
            pltpu.VMEM((2, 256, 256), jnp.float32),
            pltpu.VMEM((2 * UP, 128), jnp.float32),
            pltpu.VMEM((TOUT, n, 16, 128), jnp.float32),
            pltpu.VMEM((TOUT, n, 16, 128), jnp.float32),
            pltpu.VMEM((n * 32, 128), jnp.float32),
            dma((8,)), dma((TOUT, n)), dma((TOUT, n)), dma((TOUT,)),
            dma((TOUT, n)), dma((TOUT, n)), dma((TOUT,)),
        ],
        compiler_params=pltpu.CompilerParams(
            collective_id=0, has_side_effects=True, vmem_limit_bytes=56 << 20
        ),
    )(
        voltages, gains, feed_cyl.reshape(-1, 128), feed_ns.reshape(-1, 128),
        ew_index, ns_beam.reshape(-1, 128),
    )
    return out.transpose(1, 0, 2)


def solution(mesh):
    placed = (P(None, "chan", None, None, "grp"), P(None, None, "chan"), P(), P(), P(), P())
    n = mesh.shape["chan"]

    def part(voltages, gains, feed_cyl, feed_ns, ew_index, ns_beam):
        fits = voltages.shape == (2, 64, 2, 2 * n, UP * DS * TOUT) and n * 64 == FEEDS
        run = functools.partial(fused, n) if fits else shards
        return run(voltages, gains, feed_cyl, feed_ns, ew_index, ns_beam)

    return jax.shard_map(
        part, mesh=mesh, in_specs=placed, out_specs=P("chan", "grp", None), check_vma=False
    )
```

```python
import functools
import math

import jax
import jax.numpy as jnp
from jax import lax
from jax.experimental import pallas as pl
from jax.experimental.pallas import tpu as pltpu
from jax.sharding import PartitionSpec as P

CYL = 4
NSF = 256
EWB = 4
NSB = 256
EW_PH = 64
UP = 16
DS = 4
FEEDS = 1024
BEAMS = 1024
TOUT = 4


eps_power = 1e-06
MESH = pl.DeviceIdType.MESH


def phase_table(feed_cyl, feed_ns, ew_index, ns_beam):
    modulus = 2 * NSF * EW_PH
    cyl_onehot = (feed_cyl[:, None] == jnp.arange(CYL, dtype=jnp.int32)[None, :]).astype(jnp.int32)
    ew_term = jnp.sum(cyl_onehot[:, None, :] * ew_index[None, :, :], axis=2)
    ns_term = feed_ns[:, None] * ns_beam[None, :] * EW_PH
    steps_int = (ew_term[:, :, None] * (2 * NSF) + ns_term[:, None, :]) % modulus
    angles = steps_int.reshape(FEEDS, EWB * NSB).astype(jnp.float32) * (2.0 * math.pi / modulus)
    cosine = jnp.cos(angles).astype(jnp.bfloat16)
    sine_part = jnp.sin(angles).astype(jnp.bfloat16)
    upper_rows = jnp.concatenate([cosine, sine_part], axis=1)
    lower_rows = jnp.concatenate([-sine_part, cosine], axis=1)
    return jnp.concatenate([upper_rows, lower_rows], axis=0)


def upchannel_table():
    bin_index = jnp.arange(UP, dtype=jnp.int32)
    angles = (bin_index[:, None] * bin_index[None, :] % UP).astype(jnp.float32) * (
        2.0 * math.pi / UP
    )
    cosine = jnp.cos(angles)
    sine_part = jnp.sin(angles)
    return jnp.stack([jnp.stack([cosine, -sine_part], -1), jnp.stack([sine_part, cosine], -1)], 1)


def shards(voltages, gains, feed_cyl, feed_ns, ew_index, ns_beam):
    weights = phase_table(feed_cyl, feed_ns, ew_index, ns_beam).reshape(2, FEEDS, 2 * BEAMS)
    fine_table = upchannel_table()
    sample = voltages.astype(jnp.float32)
    gain_real = gains[0].T[:, :, None, None]
    gain_imag = gains[1].T[:, :, None, None]
    calibrated = jnp.stack(
        [
            (gain_real * sample[0] - gain_imag * sample[1]).astype(jnp.bfloat16),
            (gain_real * sample[1] + gain_imag * sample[0]).astype(jnp.bfloat16),
        ]
    )
    arrived = lax.all_to_all(calibrated, "chan", split_axis=3, concat_axis=1, tiled=True)
    pieces = arrived.shape[2]
    channels = arrived.shape[3]
    beam_sums = jnp.einsum("rfpct,rfq->pctq", arrived, weights, preferred_element_type=jnp.float32)
    beam_sums = beam_sums.reshape(pieces, channels, TOUT, DS, UP, 2, BEAMS)
    fine_bins = jnp.einsum(
        "pcudjrb,jrks->pbudcks", beam_sums, fine_table, precision=lax.Precision.HIGHEST
    )
    beam_power = jnp.sum(jnp.sum(fine_bins * fine_bins, axis=(3, 6)), axis=0)
    total_chans = beam_power.shape[2] * lax.axis_size("chan")
    band_sum = lax.psum(jnp.sum(beam_power, axis=(2, 3)), "chan")
    baseline = band_sum / (total_chans * UP)
    normed = beam_power / (baseline[:, :, None, None] + eps_power)
    intensity = lax.all_to_all(normed, "chan", split_axis=0, concat_axis=2, tiled=True)
    return intensity.reshape(intensity.shape[0], TOUT, intensity.shape[2] * UP)

def fft(values):
    size = len(values)
    if size == 1:
        return values
    even = fft(values[0::2])
    odd = fft(values[1::2])
    low, high = [], []
    for k in range(size // 2):
        er, ei = even[k]
        xr, xi = odd[k]
        if k == 0:
            tr, ti = xr, xi
        elif 4 * k == size:
            tr, ti = xi, -xr
        else:
            c = math.cos(2.0 * math.pi * k / size)
            s = math.sin(2.0 * math.pi * k / size)
            if 8 * k == size:
                tr, ti = (xr + xi) * c, (xi - xr) * c
            elif 8 * k == 3 * size:
                tr, ti = (xi - xr) * s, -(xr + xi) * s
            else:
                tr, ti = xr * c + xi * s, xi * c - xr * s
        low.append((er + tr, ei + ti))
        high.append((er - tr, ei - ti))
    return low + high


def cos_sin(steps):
    quarter = (steps + 64) >> 7
    x = (steps - (quarter << 7)).astype(jnp.float32) * (2.0 * math.pi / 512)
    y = x * x
    s = x * (1.0 + y * (-1 / 6 + y * (1 / 120 + y * (-1 / 5040 + y * (1 / 362880)))))
    c = 1.0 + y * (-0.5 + y * (1 / 24 + y * (-1 / 720 + y * (1 / 40320))))
    odd = (quarter & 1) == 1
    cosine = jnp.where(odd, s, c)
    sine = jnp.where(odd, c, s)
    cosine = jnp.where(((quarter + 1) & 2) == 2, -cosine, cosine)
    sine = jnp.where((quarter & 2) == 2, -sine, sine)
    return cosine, sine


def beam_kernel(
    n, volt_ref, gain_ref, cyl_ref, ns_ref, ew_ref, nb_ref, out_ref,
    volt, wide, spread, gcol, ccol, ncol, xin, x_ref,
    recv, wre, wim, sums, psc, pbuf, precv, turn,
    volt_sem, send_sem, recv_sem, own_sem, psend_sem, precv_sem, pown_sem,
):
    me = lax.axis_index("chan")

    def fetch(i):
        feeds = pl.ds(pl.multiple_of(i * 8, 8), 8)
        return pltpu.make_async_copy(volt_ref.at[:, feeds], volt.at[:, feeds], volt_sem.at[i])

    def begin(i, carry):
        fetch(i).start()
        return carry

    lax.fori_loop(0, 8, begin, 0)
    barrier = pltpu.get_barrier_semaphore()

    def greet(s, carry):
        pl.semaphore_signal(
            barrier, inc=1, device_id={"chan": lax.rem(me + s, n)}, device_id_type=MESH
        )
        return carry

    lax.fori_loop(1, n, greet, 0)

    row = lax.broadcasted_iota(jnp.int32, spread.shape, 0)
    take = ((row >> 2) & 1) * 256 + ((row >> 7) * DS + (row & 3)) * UP + ((row >> 3) & 15)
    lane = lax.broadcasted_iota(jnp.int32, spread.shape, 1)
    spread[...] = jnp.where(take == lane, 1.0, 0.0).astype(jnp.bfloat16)
    for r in range(2):
        for p in range(2):
            gcol[r, p] = jnp.broadcast_to(gain_ref[r, p : p + 1, :], (128, 64)).T
    def widen(i, carry):
        fetch(i).wait()
        first = pl.multiple_of(i * 8 * 2 * n, 8 * 2 * n)
        for r in range(2):
            for p in range(2):
                part = volt[r, pl.ds(pl.multiple_of(i * 8, 8), 8), p].astype(jnp.float32)
                part = part.reshape(8 * 2 * n, 256)
                for h in range(2):
                    wide[r, p, h, pl.ds(first, 8 * 2 * n), :] = part[:, h * 128 : (h + 1) * 128]
        return carry

    lax.fori_loop(0, 8, widen, 0)
    pl.semaphore_wait(barrier, n - 1)

    mine = pl.ds(pl.multiple_of(me * 128, 128), 128)

    def volt_copy(u, s):
        d = lax.rem(me + s, n)
        return pltpu.make_async_remote_copy(
            src_ref=x_ref.at[d, u],
            dst_ref=recv.at[u, :, mine],
            send_sem=send_sem.at[u, s],
            recv_sem=recv_sem.at[u, s],
            device_id={"chan": d},
            device_id_type=MESH,
        )

    def own_copy(u):
        return pltpu.make_async_copy(x_ref.at[me, u], recv.at[u, :, mine], own_sem.at[u])

    def power_copy(u, s):
        d = lax.rem(me + s, n)
        return pltpu.make_async_remote_copy(
            src_ref=pbuf.at[u, d],
            dst_ref=precv.at[u, me],
            send_sem=psend_sem.at[u, s],
            recv_sem=precv_sem.at[u, s],
            device_id={"chan": d},
            device_id_type=MESH,
        )

    def own_power(u):
        return pltpu.make_async_copy(pbuf.at[u, me], precv.at[u, me], pown_sem.at[u])

    def each(make, act, u):
        def one(s, carry):
            getattr(make(u, s), act)()
            return carry

        lax.fori_loop(1, n, one, 0)

    def produce(i, carry):
        s = lax.rem(i + n // 2, n)
        d = lax.rem(me + s, n)
        for p in range(2):
            for c in range(2):
                for h in range(2):
                    at = pl.ds(d * 2 + c, 64, stride=2 * n)
                    real = wide[0, p, h, at, :]
                    imag = wide[1, p, h, at, :]
                    gr = gcol[0, p]
                    gi = gcol[1, p]
                    cols = slice(c * 256 + h * 128, c * 256 + h * 128 + 128)
                    xin[p * 128 : p * 128 + 64, cols] = (gr * real - gi * imag).astype(jnp.bfloat16)
                    xin[p * 128 + 64 : p * 128 + 128, cols] = (gr * imag + gi * real).astype(jnp.bfloat16)
        turned = lax.dot_general(
            spread[...], xin[...], (((1,), (1,)), ((), ())), preferred_element_type=jnp.float32
        )
        rows = jnp.concatenate(
            [turned[:, :128].reshape(TOUT * UP, 1, 8, 128), turned[:, 128:].reshape(TOUT * UP, 1, 8, 128)],
            axis=1,
        )
        x_ref[d] = rows.astype(jnp.bfloat16).reshape(TOUT, UP * 16, 128)

        @pl.when(s > 0)
        def _():
            volt_copy(0, s).start()

        return carry

    lax.fori_loop(0, n, produce, 0)
    for u in range(1, TOUT):
        each(volt_copy, "start", u)
    for u in range(TOUT):
        own_copy(u).start()

    for i in range(FEEDS // 128):
        rows = slice(i * 128, (i + 1) * 128)
        ccol[rows, :] = jnp.broadcast_to(cyl_ref[i : i + 1, :], (128, 128)).T
        ncol[rows, :] = jnp.broadcast_to(ns_ref[i : i + 1, :], (128, 128)).T

    def table(s, carry):
        feeds = pl.ds(pl.multiple_of(s * 64, 64), 64)
        top = pl.ds(pl.multiple_of(s * 128, 128), 64)
        low = pl.ds(pl.multiple_of(s * 128 + 64, 64), 64)
        cyl = ccol[feeds, :]
        for h in range(2):
            slope = ncol[feeds, :] * nb_ref[h : h + 1, :]
            for e in range(EWB):
                shift = jnp.where(
                    cyl < 2,
                    jnp.where(cyl == 0, ew_ref[e, 0], ew_ref[e, 1]),
                    jnp.where(cyl == 2, ew_ref[e, 2], ew_ref[e, 3]),
                )
                cosine, sine = cos_sin((slope + shift * 8) & 511)
                cols = slice(e * NSB + h * 128, e * NSB + h * 128 + 128)
                cosine = cosine.astype(jnp.bfloat16)
                wre[top, cols] = cosine
                wim[low, cols] = cosine
                wim[top, cols] = sine.astype(jnp.bfloat16)
                wre[low, cols] = (-sine).astype(jnp.bfloat16)
        return carry

    lax.fori_loop(0, n, table, 0)
    blocks = BEAMS // 256
    left = lax.broadcasted_iota(jnp.int32, (16, 128), 1) < 64

    def finish(u):
        each(power_copy, "wait_recv", u)
        own_power(u).wait()

        def gather(src, carry):
            rows = precv[u, src]
            first = pl.multiple_of(src * 32, 32)
            turn[pl.ds(first, 16), :] = rows
            turn[pl.ds(first + 16, 16), :] = pltpu.roll(rows, 64, 1)
            return carry

        lax.fori_loop(0, n, gather, 0)
        beams = jnp.concatenate(
            [turn[i * 128 : (i + 1) * 128, :].T[:64] for i in range(n * 32 // 128)], axis=1
        )
        baseline = jnp.sum(beams, axis=1, keepdims=True) / (n * 32)
        out_ref[u] = beams / (baseline + eps_power)

    for u in range(TOUT):
        if u >= 2:
            finish(u - 2)
        each(volt_copy, "wait_recv", u)
        own_copy(u).wait()

        def block(i, carry, u=u):
            nb = lax.rem(i + me * blocks // n + blocks // 2, blocks)
            cols = pl.ds(pl.multiple_of(nb * 256, 256), 256)
            sums[0] = jnp.dot(recv[u], wre[:, cols], preferred_element_type=jnp.float32)
            sums[1] = jnp.dot(recv[u], wim[:, cols], preferred_element_type=jnp.float32)
            for lane in range(2):
                at = slice(lane * 128, (lane + 1) * 128)
                total = None
                for p in range(2):
                    bins = fft(
                        [
                            (
                                sums[0, j * 16 + p * 8 : j * 16 + p * 8 + 8, at],
                                sums[1, j * 16 + p * 8 : j * 16 + p * 8 + 8, at],
                            )
                            for j in range(UP)
                        ]
                    )
                    power = [r * r + i * i for r, i in bins]
                    total = power if p == 0 else [a + b for a, b in zip(total, power)]
                for k in range(UP):
                    part = total[k]
                    part = part + pltpu.roll(part, 6, 0)
                    part = part + pltpu.roll(part, 7, 0)
                    psc[k : k + 1, :] = part[0:1]
                    psc[UP + k : UP + k + 1, :] = part[4:5]
                c0 = psc[:UP, :]
                c1 = psc[UP:, :]
                pair = (nb * 2 + lane) * 2
                pbuf[u, pair] = jnp.where(left, c0, pltpu.roll(c1, 64, 1))
                pbuf[u, pair + 1] = jnp.where(left, pltpu.roll(c0, 64, 1), c1)
            for q in range(n // blocks):
                s = lax.rem(nb * (n // blocks) + q - me + n, n)

                @pl.when(s > 0)
                def _(s=s):
                    power_copy(u, s).start()

            return carry

        lax.fori_loop(0, blocks, block, 0)
        own_power(u).start()

    for u in range(TOUT):
        each(volt_copy, "wait_send", u)

    finish(TOUT - 2)
    finish(TOUT - 1)
    for u in range(TOUT):
        each(power_copy, "wait_send", u)


def fused(n, voltages, gains, feed_cyl, feed_ns, ew_index, ns_beam):
    vmem = pl.BlockSpec(memory_space=pltpu.VMEM)
    dma = pltpu.SemaphoreType.DMA
    out = pl.pallas_call(
        functools.partial(beam_kernel, n),
        out_shape=jax.ShapeDtypeStruct((TOUT, BEAMS // n, n * 32), jnp.float32),
        in_specs=[
            pl.BlockSpec(memory_space=pl.ANY), vmem, vmem, vmem,
            pl.BlockSpec(memory_space=pltpu.SMEM), vmem,
        ],
        out_specs=vmem,
        scratch_shapes=[
            pltpu.VMEM(voltages.shape, jnp.bfloat16),
            pltpu.VMEM((2, 2, 2, 64 * 2 * n, 128), jnp.float32),
            pltpu.VMEM((512, 512), jnp.bfloat16),
            pltpu.VMEM((2, 2, 64, 128), jnp.float32),
            pltpu.VMEM((FEEDS, 128), jnp.int32),
            pltpu.VMEM((FEEDS, 128), jnp.int32),
            pltpu.VMEM((256, 512), jnp.bfloat16),
            pltpu.VMEM((n, TOUT, 256, 128), jnp.bfloat16),
            pltpu.VMEM((TOUT, 256, n * 128), jnp.bfloat16),
            pltpu.VMEM((2 * FEEDS, BEAMS), jnp.bfloat16),
            pltpu.VMEM((2 * FEEDS, BEAMS), jnp.bfloat16),
            pltpu.VMEM((2, 256, 256), jnp.float32),
            pltpu.VMEM((2 * UP, 128), jnp.float32),
            pltpu.VMEM((TOUT, n, 16, 128), jnp.float32),
            pltpu.VMEM((TOUT, n, 16, 128), jnp.float32),
            pltpu.VMEM((n * 32, 128), jnp.float32),
            dma((8,)), dma((TOUT, n)), dma((TOUT, n)), dma((TOUT,)),
            dma((TOUT, n)), dma((TOUT, n)), dma((TOUT,)),
        ],
        compiler_params=pltpu.CompilerParams(
            collective_id=0, has_side_effects=True, vmem_limit_bytes=56 << 20
        ),
    )(
        voltages, gains, feed_cyl.reshape(-1, 128), feed_ns.reshape(-1, 128),
        ew_index, ns_beam.reshape(-1, 128),
    )
    return out.transpose(1, 0, 2)


def solution(mesh):
    placed = (P(None, "chan", None, None, "grp"), P(None, None, "chan"), P(), P(), P(), P())
    n = mesh.shape["chan"]

    def part(voltages, gains, feed_cyl, feed_ns, ew_index, ns_beam):
        fits = voltages.shape == (2, 64, 2, 2 * n, UP * DS * TOUT) and n * 64 == FEEDS
        run = functools.partial(fused, n) if fits else shards
        return run(voltages, gains, feed_cyl, feed_ns, ew_index, ns_beam)

    return jax.shard_map(
        part, mesh=mesh, in_specs=placed, out_specs=P("chan", "grp", None), check_vma=False
    )
```

```python
import functools
import math

import jax
import jax.numpy as jnp
from jax import lax
from jax.experimental import pallas as pl
from jax.experimental.pallas import tpu as pltpu
from jax.sharding import PartitionSpec as P

CYL = 4
NSF = 256
EWB = 4
NSB = 256
EW_PH = 64
UP = 16
DS = 4
FEEDS = 1024
BEAMS = 1024
TOUT = 4


eps_power = 1e-06
MESH = pl.DeviceIdType.MESH


def phase_table(feed_cyl, feed_ns, ew_index, ns_beam):
    modulus = 2 * NSF * EW_PH
    cyl_onehot = (feed_cyl[:, None] == jnp.arange(CYL, dtype=jnp.int32)[None, :]).astype(jnp.int32)
    ew_term = jnp.sum(cyl_onehot[:, None, :] * ew_index[None, :, :], axis=2)
    ns_term = feed_ns[:, None] * ns_beam[None, :] * EW_PH
    steps_int = (ew_term[:, :, None] * (2 * NSF) + ns_term[:, None, :]) % modulus
    angles = steps_int.reshape(FEEDS, EWB * NSB).astype(jnp.float32) * (2.0 * math.pi / modulus)
    cosine = jnp.cos(angles).astype(jnp.bfloat16)
    sine_part = jnp.sin(angles).astype(jnp.bfloat16)
    upper_rows = jnp.concatenate([cosine, sine_part], axis=1)
    lower_rows = jnp.concatenate([-sine_part, cosine], axis=1)
    return jnp.concatenate([upper_rows, lower_rows], axis=0)


def upchannel_table():
    bin_index = jnp.arange(UP, dtype=jnp.int32)
    angles = (bin_index[:, None] * bin_index[None, :] % UP).astype(jnp.float32) * (
        2.0 * math.pi / UP
    )
    cosine = jnp.cos(angles)
    sine_part = jnp.sin(angles)
    return jnp.stack([jnp.stack([cosine, -sine_part], -1), jnp.stack([sine_part, cosine], -1)], 1)


def shards(voltages, gains, feed_cyl, feed_ns, ew_index, ns_beam):
    weights = phase_table(feed_cyl, feed_ns, ew_index, ns_beam).reshape(2, FEEDS, 2 * BEAMS)
    fine_table = upchannel_table()
    sample = voltages.astype(jnp.float32)
    gain_real = gains[0].T[:, :, None, None]
    gain_imag = gains[1].T[:, :, None, None]
    calibrated = jnp.stack(
        [
            (gain_real * sample[0] - gain_imag * sample[1]).astype(jnp.bfloat16),
            (gain_real * sample[1] + gain_imag * sample[0]).astype(jnp.bfloat16),
        ]
    )
    arrived = lax.all_to_all(calibrated, "chan", split_axis=3, concat_axis=1, tiled=True)
    pieces = arrived.shape[2]
    channels = arrived.shape[3]
    beam_sums = jnp.einsum("rfpct,rfq->pctq", arrived, weights, preferred_element_type=jnp.float32)
    beam_sums = beam_sums.reshape(pieces, channels, TOUT, DS, UP, 2, BEAMS)
    fine_bins = jnp.einsum(
        "pcudjrb,jrks->pbudcks", beam_sums, fine_table, precision=lax.Precision.HIGHEST
    )
    beam_power = jnp.sum(jnp.sum(fine_bins * fine_bins, axis=(3, 6)), axis=0)
    total_chans = beam_power.shape[2] * lax.axis_size("chan")
    band_sum = lax.psum(jnp.sum(beam_power, axis=(2, 3)), "chan")
    baseline = band_sum / (total_chans * UP)
    normed = beam_power / (baseline[:, :, None, None] + eps_power)
    intensity = lax.all_to_all(normed, "chan", split_axis=0, concat_axis=2, tiled=True)
    return intensity.reshape(intensity.shape[0], TOUT, intensity.shape[2] * UP)

def fft(values):
    size = len(values)
    if size == 1:
        return values
    even = fft(values[0::2])
    odd = fft(values[1::2])
    low, high = [], []
    for k in range(size // 2):
        er, ei = even[k]
        xr, xi = odd[k]
        if k == 0:
            tr, ti = xr, xi
        elif 4 * k == size:
            tr, ti = xi, -xr
        else:
            c = math.cos(2.0 * math.pi * k / size)
            s = math.sin(2.0 * math.pi * k / size)
            if 8 * k == size:
                tr, ti = (xr + xi) * c, (xi - xr) * c
            elif 8 * k == 3 * size:
                tr, ti = (xi - xr) * s, -(xr + xi) * s
            else:
                tr, ti = xr * c + xi * s, xi * c - xr * s
        low.append((er + tr, ei + ti))
        high.append((er - tr, ei - ti))
    return low + high


def cos_sin(steps):
    quarter = (steps + 64) >> 7
    x = (steps - (quarter << 7)).astype(jnp.float32) * (2.0 * math.pi / 512)
    y = x * x
    s = x * (1.0 + y * (-1 / 6 + y * (1 / 120 + y * (-1 / 5040 + y * (1 / 362880)))))
    c = 1.0 + y * (-0.5 + y * (1 / 24 + y * (-1 / 720 + y * (1 / 40320))))
    odd = (quarter & 1) == 1
    cosine = jnp.where(odd, s, c)
    sine = jnp.where(odd, c, s)
    cosine = jnp.where(((quarter + 1) & 2) == 2, -cosine, cosine)
    sine = jnp.where((quarter & 2) == 2, -sine, sine)
    return cosine, sine


def beam_kernel(
    n, volt_ref, gain_ref, cyl_ref, ns_ref, ew_ref, nb_ref, out_ref,
    volt, wide, spread, gcol, ccol, ncol, xin, x_ref,
    recv, wre, wim, sums, psc, pbuf, precv, turn,
    volt_sem, send_sem, recv_sem, own_sem, psend_sem, precv_sem, pown_sem,
):
    me = lax.axis_index("chan")

    def fetch(i):
        feeds = pl.ds(pl.multiple_of(i * 8, 8), 8)
        return pltpu.make_async_copy(volt_ref.at[:, feeds], volt.at[:, feeds], volt_sem.at[i])

    def begin(i, carry):
        fetch(i).start()
        return carry

    lax.fori_loop(0, 8, begin, 0)
    barrier = pltpu.get_barrier_semaphore()

    def greet(s, carry):
        pl.semaphore_signal(
            barrier, inc=1, device_id={"chan": lax.rem(me + s, n)}, device_id_type=MESH
        )
        return carry

    lax.fori_loop(1, n, greet, 0)

    row = lax.broadcasted_iota(jnp.int32, spread.shape, 0)
    take = ((row >> 2) & 1) * 256 + ((row >> 7) * DS + (row & 3)) * UP + ((row >> 3) & 15)
    lane = lax.broadcasted_iota(jnp.int32, spread.shape, 1)
    spread[...] = jnp.where(take == lane, 1.0, 0.0).astype(jnp.bfloat16)
    for r in range(2):
        for p in range(2):
            gcol[r, p] = jnp.broadcast_to(gain_ref[r, p : p + 1, :], (128, 64)).T
    def widen(i, carry):
        fetch(i).wait()
        first = pl.multiple_of(i * 8 * 2 * n, 8 * 2 * n)
        for r in range(2):
            for p in range(2):
                part = volt[r, pl.ds(pl.multiple_of(i * 8, 8), 8), p].astype(jnp.float32)
                part = part.reshape(8 * 2 * n, 256)
                for h in range(2):
                    wide[r, p, h, pl.ds(first, 8 * 2 * n), :] = part[:, h * 128 : (h + 1) * 128]
        return carry

    lax.fori_loop(0, 8, widen, 0)
    pl.semaphore_wait(barrier, n - 1)

    mine = pl.ds(pl.multiple_of(me * 128, 128), 128)

    def volt_copy(u, s):
        d = lax.rem(me + s, n)
        return pltpu.make_async_remote_copy(
            src_ref=x_ref.at[d, u],
            dst_ref=recv.at[u, :, mine],
            send_sem=send_sem.at[u, s],
            recv_sem=recv_sem.at[u, s],
            device_id={"chan": d},
            device_id_type=MESH,
        )

    def own_copy(u):
        return pltpu.make_async_copy(x_ref.at[me, u], recv.at[u, :, mine], own_sem.at[u])

    def power_copy(u, s):
        d = lax.rem(me + s, n)
        return pltpu.make_async_remote_copy(
            src_ref=pbuf.at[u, d],
            dst_ref=precv.at[u, me],
            send_sem=psend_sem.at[u, s],
            recv_sem=precv_sem.at[u, s],
            device_id={"chan": d},
            device_id_type=MESH,
        )

    def own_power(u):
        return pltpu.make_async_copy(pbuf.at[u, me], precv.at[u, me], pown_sem.at[u])

    def each(make, act, u):
        def one(s, carry):
            getattr(make(u, s), act)()
            return carry

        lax.fori_loop(1, n, one, 0)

    def produce(i, carry):
        s = lax.rem(i + 1, n)
        d = lax.rem(me + s, n)
        for p in range(2):
            for c in range(2):
                for h in range(2):
                    at = pl.ds(d * 2 + c, 64, stride=2 * n)
                    real = wide[0, p, h, at, :]
                    imag = wide[1, p, h, at, :]
                    gr = gcol[0, p]
                    gi = gcol[1, p]
                    cols = slice(c * 256 + h * 128, c * 256 + h * 128 + 128)
                    xin[p * 128 : p * 128 + 64, cols] = (gr * real - gi * imag).astype(jnp.bfloat16)
                    xin[p * 128 + 64 : p * 128 + 128, cols] = (gr * imag + gi * real).astype(jnp.bfloat16)
        turned = lax.dot_general(
            spread[...], xin[...], (((1,), (1,)), ((), ())), preferred_element_type=jnp.float32
        )
        rows = jnp.concatenate(
            [turned[:, :128].reshape(TOUT * UP, 1, 8, 128), turned[:, 128:].reshape(TOUT * UP, 1, 8, 128)],
            axis=1,
        )
        x_ref[d] = rows.astype(jnp.bfloat16).reshape(TOUT, UP * 16, 128)

        @pl.when(s > 0)
        def _():
            volt_copy(0, s).start()

        return carry

    lax.fori_loop(0, n, produce, 0)
    for u in range(1, TOUT):
        each(volt_copy, "start", u)
    for u in range(TOUT):
        own_copy(u).start()

    for i in range(FEEDS // 128):
        rows = slice(i * 128, (i + 1) * 128)
        ccol[rows, :] = jnp.broadcast_to(cyl_ref[i : i + 1, :], (128, 128)).T
        ncol[rows, :] = jnp.broadcast_to(ns_ref[i : i + 1, :], (128, 128)).T

    def table(s, carry):
        feeds = pl.ds(pl.multiple_of(s * 64, 64), 64)
        top = pl.ds(pl.multiple_of(s * 128, 128), 64)
        low = pl.ds(pl.multiple_of(s * 128 + 64, 64), 64)
        cyl = ccol[feeds, :]
        for h in range(2):
            slope = ncol[feeds, :] * nb_ref[h : h + 1, :]
            for e in range(EWB):
                shift = jnp.where(
                    cyl < 2,
                    jnp.where(cyl == 0, ew_ref[e, 0], ew_ref[e, 1]),
                    jnp.where(cyl == 2, ew_ref[e, 2], ew_ref[e, 3]),
                )
                cosine, sine = cos_sin((slope + shift * 8) & 511)
                cols = slice(e * NSB + h * 128, e * NSB + h * 128 + 128)
                cosine = cosine.astype(jnp.bfloat16)
                wre[top, cols] = cosine
                wim[low, cols] = cosine
                wim[top, cols] = sine.astype(jnp.bfloat16)
                wre[low, cols] = (-sine).astype(jnp.bfloat16)
        return carry

    lax.fori_loop(0, n, table, 0)
    blocks = BEAMS // 256
    left = lax.broadcasted_iota(jnp.int32, (16, 128), 1) < 64

    for u in range(TOUT):
        each(volt_copy, "wait_recv", u)
        own_copy(u).wait()

        def block(i, carry, u=u):
            nb = lax.rem(i + me * blocks // n + blocks // 2, blocks)
            cols = pl.ds(pl.multiple_of(nb * 256, 256), 256)
            sums[0] = jnp.dot(recv[u], wre[:, cols], preferred_element_type=jnp.float32)
            sums[1] = jnp.dot(recv[u], wim[:, cols], preferred_element_type=jnp.float32)
            for lane in range(2):
                at = slice(lane * 128, (lane + 1) * 128)
                total = None
                for p in range(2):
                    bins = fft(
                        [
                            (
                                sums[0, j * 16 + p * 8 : j * 16 + p * 8 + 8, at],
                                sums[1, j * 16 + p * 8 : j * 16 + p * 8 + 8, at],
                            )
                            for j in range(UP)
                        ]
                    )
                    power = [r * r + i * i for r, i in bins]
                    total = power if p == 0 else [a + b for a, b in zip(total, power)]
                for k in range(UP):
                    part = total[k]
                    part = part + pltpu.roll(part, 6, 0)
                    part = part + pltpu.roll(part, 7, 0)
                    psc[k : k + 1, :] = part[0:1]
                    psc[UP + k : UP + k + 1, :] = part[4:5]
                c0 = psc[:UP, :]
                c1 = psc[UP:, :]
                pair = (nb * 2 + lane) * 2
                pbuf[u, pair] = jnp.where(left, c0, pltpu.roll(c1, 64, 1))
                pbuf[u, pair + 1] = jnp.where(left, pltpu.roll(c0, 64, 1), c1)
            for q in range(n // blocks):
                s = lax.rem(nb * (n // blocks) + q - me + n, n)

                @pl.when(s > 0)
                def _(s=s):
                    power_copy(u, s).start()

            return carry

        lax.fori_loop(0, blocks, block, 0)
        own_power(u).start()

    for u in range(TOUT):
        each(volt_copy, "wait_send", u)

    for u in range(TOUT):
        each(power_copy, "wait_recv", u)
        own_power(u).wait()

        def gather(src, carry, u=u):
            rows = precv[u, src]
            first = pl.multiple_of(src * 32, 32)
            turn[pl.ds(first, 16), :] = rows
            turn[pl.ds(first + 16, 16), :] = pltpu.roll(rows, 64, 1)
            return carry

        lax.fori_loop(0, n, gather, 0)
        beams = jnp.concatenate(
            [turn[i * 128 : (i + 1) * 128, :].T[:64] for i in range(n * 32 // 128)], axis=1
        )
        baseline = jnp.sum(beams, axis=1, keepdims=True) / (n * 32)
        out_ref[u] = beams / (baseline + eps_power)
    for u in range(TOUT):
        each(power_copy, "wait_send", u)


def fused(n, voltages, gains, feed_cyl, feed_ns, ew_index, ns_beam):
    vmem = pl.BlockSpec(memory_space=pltpu.VMEM)
    dma = pltpu.SemaphoreType.DMA
    out = pl.pallas_call(
        functools.partial(beam_kernel, n),
        out_shape=jax.ShapeDtypeStruct((TOUT, BEAMS // n, n * 32), jnp.float32),
        in_specs=[
            pl.BlockSpec(memory_space=pl.ANY), vmem, vmem, vmem,
            pl.BlockSpec(memory_space=pltpu.SMEM), vmem,
        ],
        out_specs=vmem,
        scratch_shapes=[
            pltpu.VMEM(voltages.shape, jnp.bfloat16),
            pltpu.VMEM((2, 2, 2, 64 * 2 * n, 128), jnp.float32),
            pltpu.VMEM((512, 512), jnp.bfloat16),
            pltpu.VMEM((2, 2, 64, 128), jnp.float32),
            pltpu.VMEM((FEEDS, 128), jnp.int32),
            pltpu.VMEM((FEEDS, 128), jnp.int32),
            pltpu.VMEM((256, 512), jnp.bfloat16),
            pltpu.VMEM((n, TOUT, 256, 128), jnp.bfloat16),
            pltpu.VMEM((TOUT, 256, n * 128), jnp.bfloat16),
            pltpu.VMEM((2 * FEEDS, BEAMS), jnp.bfloat16),
            pltpu.VMEM((2 * FEEDS, BEAMS), jnp.bfloat16),
            pltpu.VMEM((2, 256, 256), jnp.float32),
            pltpu.VMEM((2 * UP, 128), jnp.float32),
            pltpu.VMEM((TOUT, n, 16, 128), jnp.float32),
            pltpu.VMEM((TOUT, n, 16, 128), jnp.float32),
            pltpu.VMEM((n * 32, 128), jnp.float32),
            dma((8,)), dma((TOUT, n)), dma((TOUT, n)), dma((TOUT,)),
            dma((TOUT, n)), dma((TOUT, n)), dma((TOUT,)),
        ],
        compiler_params=pltpu.CompilerParams(
            collective_id=0, has_side_effects=True, vmem_limit_bytes=56 << 20
        ),
    )(
        voltages, gains, feed_cyl.reshape(-1, 128), feed_ns.reshape(-1, 128),
        ew_index, ns_beam.reshape(-1, 128),
    )
    return out.transpose(1, 0, 2)


def solution(mesh):
    placed = (P(None, "chan", None, None, "grp"), P(None, None, "chan"), P(), P(), P(), P())
    n = mesh.shape["chan"]

    def part(voltages, gains, feed_cyl, feed_ns, ew_index, ns_beam):
        fits = voltages.shape == (2, 64, 2, 2 * n, UP * DS * TOUT) and n * 64 == FEEDS
        run = functools.partial(fused, n) if fits else shards
        return run(voltages, gains, feed_cyl, feed_ns, ew_index, ns_beam)

    return jax.shard_map(
        part, mesh=mesh, in_specs=placed, out_specs=P("chan", "grp", None), check_vma=False
    )
```
